512 devices in a mesh: ctx: 32 (over z, core), dp: 16 (over x, y).
Axes of the slice: x: 4, y: 4, z: 16, core: 2. Of those that a mesh axis runs over, the one named last changes fastest.
Arguments:
- q_nope: bfloat16 [4096, 16384], P('ctx', 'dp'), may hold values from -6 to 6
- q_rope: bfloat16 [4096, 8192], P('ctx', 'dp'), may hold values from -400 to 400
- latent: bfloat16 [4096, 512], P('ctx'), may hold values from -6 to 6
- k_rope: bfloat16 [4096, 64], P('ctx'), may hold values from -5.2 to 5.2
- w_uk: bfloat16 [512, 16384], P('ctx', 'dp'), may hold values from -0.25 to 0.25
- w_uv: bfloat16 [512, 16384], P('ctx', 'dp'), may hold values from -0.25 to 0.25
- out_grad: bfloat16 [4096, 16384], P('ctx', 'dp'), may hold values from -6 to 6
- log_prob: float32 [4096], P('ctx'), may hold values from -5.4 to 0
- ref_logp: float32 [1], replicated, may hold values from -2.5 to -0.5
- doc_ids: int32 [4096], P('ctx'), may hold values from 0 to 31, never falling along the last dimension, each value on 1 to 256 neighbouring positions
- loss_mask: int32 [4096], P('ctx'), may hold values from 0 to 1, as said below
Outputs:
- dq_nope: bfloat16 [4096, 16384], P('ctx', 'dp')
- dq_rope: bfloat16 [4096, 8192], P('ctx', 'dp')
- d_latent: bfloat16 [4096, 512], P('ctx')
- d_krope: bfloat16 [4096, 64], P('ctx')
- dw_uk: float32 [512, 16384], P('ctx', 'dp')
- dw_uv: float32 [512, 16384], P('ctx', 'dp')
The draws below stay inside these ranges and needn't reach their ends.
Inputs may be any that keep to these rules, and one draw needn't show every extreme that they name: `doc_ids`: each document is a run of consecutive positions of at most 256 tokens; numbers never fall along the sequence. `loss_mask`: the last token of the sequence counts.
All inputs are finite; a program needn't handle non-finite values.
Results may differ from the reference program's by a relative error of at most 0.03.
Values may be sent and summed in bfloat16 or wider, within the bound.
A program may use at most 64 MiB of HBM per device.

```python
import math
import jax
import jax.numpy as jnp
import numpy as np
from jax import lax

HEADS = 128
LAT = 512
NOPE = 128
ROPE = 64
VDIM = 128
Q_DEV = 128
SEQ = 4096
DOC_MOST = 256
DOCS = 32


def rope_pair(key):
    base_keys = jax.random.normal(jax.random.fold_in(key, 11), (SEQ, ROPE), jnp.float32)
    base_keys = jnp.clip(base_keys, -5.0, 5.0)
    base_query = jax.random.normal(jax.random.fold_in(key, 23), (SEQ, HEADS, ROPE), jnp.float32)
    base_query = jnp.clip(base_query, -6.0, 6.0)
    rope_keys = base_keys
    queries = base_query
    return (rope_keys, queries.reshape(SEQ, HEADS * ROPE))


def draw_k_rope(key, part):
    return rope_pair(key)[0].astype(jnp.bfloat16)


def draw_q_rope(key, part):
    return rope_pair(key)[1].astype(jnp.bfloat16)


def draw_log_prob(key, part):
    position = jnp.arange(SEQ).astype(jnp.float32) / SEQ
    level = jax.random.uniform(jax.random.fold_in(key, 5), (), jnp.float32, 0.5, 1.5)
    spread = jax.random.uniform(jax.random.fold_in(key, 7), (SEQ,), jnp.float32, 0.5, 1.5)
    return -(0.3 + 1.7 * position) * level * spread


def draw_loss_mask(key, part):
    position = jnp.arange(SEQ)
    ticket = jax.random.randint(key, (SEQ,), 0, 1000)
    chosen = ticket < 200 + 700 * position // SEQ
    chosen = chosen | (position == SEQ - 1)
    return chosen.astype(jnp.int32)


def block_scale(stream_key, extent, split, least, top_value):
    loudness, own = 1.0, jax.random.fold_in(stream_key, 6)
    for dim, parts in split:
        draws = jnp.exp(jax.random.uniform(jax.random.fold_in(own, dim), (parts,), jnp.float32, least / len(split), top_value / len(split)))
        loudness = loudness * jnp.repeat(draws, extent[dim] // parts).reshape([-1 if axis == dim else 1 for axis in range(len(extent))])
    return loudness


def length_profile(amount, total, limit, slope):
    portions = [(1 << 20) // math.isqrt(grade ** slope) + 1 for grade in range(2, amount + 1)]
    rest, given = total - limit - (amount - 1), [1] * (amount - 1)
    while rest > 0:
        movable = [i for i in range(amount - 1) if given[i] < limit]
        pool, budget = sum([portions[i] for i in movable]), rest
        for i in movable:
            extra = min(limit - given[i], max(1, budget * portions[i] // pool), rest)
            given[i] = given[i] + extra
            rest = rest - extra
    return np.array([limit] + given)


def ragged(own_key, number_of, total, reach, slope):
    if number_of == 2:
        one = jax.random.randint(own_key, (), max(1, total - reach), min(reach, total - 1) + 1)
        return jnp.stack([one, total - one])
    sizes = jnp.asarray(length_profile(number_of, total, reach, slope), jnp.int32)
    pairs = (number_of - 1) // 2
    donor, receiver = sizes[1:1 + 2 * pairs:2], sizes[2:2 + 2 * pairs:2]
    room = jnp.minimum(donor - 1, reach - receiver)
    moved = jax.random.randint(jax.random.fold_in(own_key, 1), (pairs,), 0, 1 << 20) % (room + 1)
    sizes = sizes.at[1:1 + 2 * pairs:2].set(donor - moved).at[2:2 + 2 * pairs:2].set(receiver + moved)
    return sizes[jax.random.permutation(jax.random.fold_in(own_key, 2), number_of)]


def scatter_about(key, shape, scale, reach, shards=(), kind=jnp.bfloat16):
    drawn = jax.random.normal(key, shape, jnp.float32) * scale
    if len(shards) > 0:
        drawn = block_scale(key, shape, shards, -0.22, 0.18) * drawn
    return jnp.clip(drawn, min=-reach, max=reach).astype(kind)


def setup_inputs(seed: int = 0) -> dict:
    splits = jax.random.split(jax.random.key(seed), 12)
    q_nope = scatter_about(splits[0], (SEQ, HEADS * NOPE), 1.0, 6.0, ((0, 32), (1, 16)))
    q_rope = draw_q_rope(jax.random.fold_in(splits[11], 71), 0)
    latent = scatter_about(splits[2], (SEQ, LAT), 1.0, 6.0, ((0, 32),))
    k_rope = draw_k_rope(jax.random.fold_in(splits[11], 71), 0)
    w_uk = scatter_about(splits[4], (LAT, HEADS * NOPE), LAT ** -0.5, 0.25, ((0, 32), (1, 16)))
    w_uv = scatter_about(splits[5], (LAT, HEADS * VDIM), LAT ** -0.5, 0.25, ((0, 32), (1, 16)))
    out_grad = scatter_about(splits[6], (SEQ, HEADS * VDIM), 1.0, 6.0, ((0, 32), (1, 16)))
    log_prob = draw_log_prob(jax.random.fold_in(splits[11], 71), 0)
    ref_logp = jnp.clip(jax.random.uniform(splits[8], (1,), jnp.float32, -2.5, -0.5), -2.5, -0.5)
    doc_ids = jnp.searchsorted(jnp.cumsum(ragged(splits[9], DOCS, SEQ, DOC_MOST, 2)), jnp.arange(SEQ), side="right").astype(jnp.int32)
    loss_mask = draw_loss_mask(jax.random.fold_in(splits[11], 71), 0)
    return dict(q_nope=q_nope, q_rope=q_rope, latent=latent, k_rope=k_rope, w_uk=w_uk, w_uv=w_uv, out_grad=out_grad, log_prob=log_prob, ref_logp=ref_logp, doc_ids=doc_ids, loss_mask=loss_mask)


npo_beta = 1.0

def attend(query_nope, query_rope, key_nope, key_rope, values, grad_out, allowed):
    single = jnp.float32
    score_scale = 1.0 / math.sqrt(NOPE + ROPE)
    scores = jnp.einsum('qhd,khd->hqk', query_nope.astype(single), key_nope.astype(single))
    scores = scores + jnp.einsum('qhd,kd->hqk', query_rope.astype(single), key_rope.astype(single))
    scores = jnp.where(allowed[None], scores * score_scale, -1e+30)
    row_max = lax.optimization_barrier(jnp.max(scores, axis=2, keepdims=True))
    expon = jnp.where(allowed[None], jnp.exp(scores - row_max), 0.0)
    probs = expon / lax.optimization_barrier(jnp.sum(expon, axis=2, keepdims=True))
    probs_low = probs.astype(jnp.bfloat16)
    attn_out = jnp.einsum('hqk,khd->hqd', probs_low.astype(single), values.astype(single))
    delta = jnp.einsum('hqd,qhd->hq', attn_out, grad_out.astype(single))
    dprob = jnp.einsum('qhd,khd->hqk', grad_out.astype(single), values.astype(single))
    dscore = (probs * (dprob - delta[:, :, None]) * score_scale).astype(jnp.bfloat16)
    dscore_f = dscore.astype(single)
    dq_nope = jnp.einsum('hqk,khd->qhd', dscore_f, key_nope.astype(single)).astype(jnp.bfloat16)
    dq_rope = jnp.einsum('hqk,kd->qhd', dscore_f, key_rope.astype(single)).astype(jnp.bfloat16)
    part_nope = jnp.einsum('hqk,qhd->khd', dscore_f, query_nope.astype(single)).astype(jnp.bfloat16)
    part_rope = jnp.einsum('hqk,qhd->kd', dscore_f, query_rope.astype(single)).astype(jnp.bfloat16)
    part_value = jnp.einsum('hqk,qhd->khd', probs_low.astype(single), grad_out.astype(single)).astype(jnp.bfloat16)
    return (dq_nope, dq_rope, part_nope, part_value, part_rope)

def reference(q_nope, q_rope, latent, k_rope, w_uk, w_uv, out_grad, log_prob, ref_logp, doc_ids, loss_mask):
    width_nope = w_uk.shape[1]
    width_value = w_uv.shape[1]
    head_count = width_nope // NOPE
    seq_len = latent.shape[0]
    lat_width = latent.shape[1]
    blocks = seq_len // Q_DEV
    margin = 2 * Q_DEV
    highest = lax.Precision.HIGHEST
    key_nope = jnp.dot(latent, w_uk, preferred_element_type=jnp.float32).astype(jnp.bfloat16)
    values = jnp.dot(latent, w_uv, preferred_element_type=jnp.float32).astype(jnp.bfloat16)
    mask_f = loss_mask.astype(jnp.float32)
    live_count = jnp.sum(mask_f)
    mean_logp = jnp.sum(mask_f * log_prob) / live_count
    npo_weight = 2.0 * jax.nn.sigmoid(npo_beta * (mean_logp - ref_logp[0])) * seq_len / live_count
    grad_out = (npo_weight * mask_f[:, None] * out_grad.astype(jnp.float32)).astype(jnp.bfloat16)
    pad_nope = jnp.concatenate([jnp.zeros((margin, width_nope), jnp.bfloat16), key_nope], axis=0)
    pad_value = jnp.concatenate([jnp.zeros((margin, width_value), jnp.bfloat16), values], axis=0)
    pad_rope = jnp.concatenate([jnp.zeros((margin, ROPE), jnp.bfloat16), k_rope], axis=0)
    pad_latent = jnp.concatenate([jnp.zeros((margin, lat_width), jnp.bfloat16), latent], axis=0)
    pad_docs = jnp.concatenate([jnp.full((margin,), -1, jnp.int32), doc_ids.astype(jnp.int32)], axis=0)
    query_idx = jnp.arange(Q_DEV, dtype=jnp.int32)
    key_idx = jnp.arange(3 * Q_DEV, dtype=jnp.int32)
    uk_t = w_uk.astype(jnp.float32).T
    uv_t = w_uv.astype(jnp.float32).T

    def one_block(carry, block_id):
        lat_acc, rope_acc, weight_acc = carry
        first_row = (block_id * Q_DEV).astype(jnp.int32)
        query_nope = lax.dynamic_slice_in_dim(q_nope, first_row, Q_DEV, 0).reshape(Q_DEV, head_count, NOPE)
        query_rope = lax.dynamic_slice_in_dim(q_rope, first_row, Q_DEV, 0).reshape(Q_DEV, head_count, ROPE)
        block_grad = lax.dynamic_slice_in_dim(grad_out, first_row, Q_DEV, 0).reshape(Q_DEV, head_count, VDIM)
        query_docs = lax.dynamic_slice_in_dim(doc_ids.astype(jnp.int32), first_row, Q_DEV, 0)
        win_nope = lax.dynamic_slice_in_dim(pad_nope, first_row, 3 * Q_DEV, 0).reshape(3 * Q_DEV, head_count, NOPE)
        win_value = lax.dynamic_slice_in_dim(pad_value, first_row, 3 * Q_DEV, 0).reshape(3 * Q_DEV, head_count, VDIM)
        win_rope = lax.dynamic_slice_in_dim(pad_rope, first_row, 3 * Q_DEV, 0)
        win_docs = lax.dynamic_slice_in_dim(pad_docs, first_row, 3 * Q_DEV, 0)
        win_latent = lax.dynamic_slice_in_dim(pad_latent, first_row, 3 * Q_DEV, 0).astype(jnp.float32)
        allowed = (query_docs[:, None] == win_docs[None, :]) & (key_idx[None, :] - margin <= query_idx[:, None])
        dq_nope, dq_rope, part_nope, part_value, part_rope = attend(query_nope, query_rope, win_nope, win_rope, win_value, block_grad, allowed)
        nope_f = part_nope.reshape(3 * Q_DEV, width_nope).astype(jnp.float32)
        value_f = part_value.reshape(3 * Q_DEV, width_value).astype(jnp.float32)
        lat_term = jnp.dot(nope_f, uk_t, precision=highest) + jnp.dot(value_f, uv_t, precision=highest)
        lat_old = lax.dynamic_slice_in_dim(lat_acc, first_row, 3 * Q_DEV, 0)
        lat_acc = lax.dynamic_update_slice_in_dim(lat_acc, lat_old + lat_term, first_row, 0)
        rope_old = lax.dynamic_slice_in_dim(rope_acc, first_row, 3 * Q_DEV, 0)
        rope_acc = lax.dynamic_update_slice_in_dim(rope_acc, rope_old + part_rope.astype(jnp.float32), first_row, 0)
        both = jnp.concatenate([nope_f, value_f], axis=1)
        weight_acc = weight_acc + jnp.dot(win_latent.T, both, precision=highest)
        return ((lat_acc, rope_acc, weight_acc), (dq_nope.reshape(Q_DEV, width_nope), dq_rope.reshape(Q_DEV, head_count * ROPE)))
    start = (jnp.zeros((seq_len + margin, lat_width), jnp.float32), jnp.zeros((seq_len + margin, ROPE), jnp.float32), jnp.zeros((lat_width, width_nope + width_value), jnp.float32))
    final, stacked = lax.scan(one_block, start, jnp.arange(blocks, dtype=jnp.int32))
    lat_acc, rope_acc, weight_acc = final
    dq_nope = stacked[0].reshape(seq_len, width_nope)
    dq_rope = stacked[1].reshape(seq_len, head_count * ROPE)
    d_latent = lat_acc[margin:].astype(jnp.bfloat16)
    d_krope = rope_acc[margin:].astype(jnp.bfloat16)
    return (dq_nope, dq_rope, d_latent, d_krope, weight_acc[:, :width_nope], weight_acc[:, width_nope:])
```

```python
import math

import jax
import jax.numpy as jnp
from jax import lax
from jax.experimental import pallas as pl
from jax.experimental.pallas import tpu as pltpu
from jax.sharding import PartitionSpec as P

NOPE = 128
ROPE = 64
npo_beta = 1.0
MESH = pl.DeviceIdType.MESH
RIGHT = (8, 7, 8)
LEFT = (7, 8, 7)
VMEM = pl.BlockSpec(memory_space=pltpu.VMEM)
f32 = jnp.float32
bf16 = jnp.bfloat16


def greet(peers):
    barrier = pltpu.get_barrier_semaphore()
    for peer in peers:
        pl.semaphore_signal(barrier, inc=1, device_id=peer, device_id_type=MESH)
    pl.semaphore_wait(barrier, len(peers))


def remote(src, dst, send, recv, peer):
    return pltpu.make_async_remote_copy(
        src_ref=src, dst_ref=dst, send_sem=send, recv_sem=recv, device_id=peer, device_id_type=MESH
    )


def loop(first, last, body):
    def step(s, carry):
        body(s)
        return carry

    lax.fori_loop(first, last, step, 0)


def gather_kernel(
    uk_ref, uv_ref, st_ref, h_ref, buk, buv, bst, win,
    own_sem, ring_send, ring_recv, par_send, par_recv, halo_send, halo_recv,
):
    me = lax.axis_index("ctx")
    n = 32
    right, left = lax.rem(me + 2, n), lax.rem(me + n - 2, n)
    partner = me + 1 - 2 * lax.rem(me, 2)
    ring_peer = ({"ctx": right}, {"ctx": left})
    mate = {"ctx": partner}
    near = {"ctx": lax.rem(me + 1, n)}
    srcs, bufs = (uk_ref, uv_ref, st_ref), (buk, buv, bst)
    counts = (RIGHT, LEFT)

    def index(base, way, s):
        return lax.rem(base + n - 2 * s, n) if way == 0 else lax.rem(base + 2 * s, n)

    def ring(i, way, s):
        slot = bufs[i].at[index(me, way, s)]
        src = srcs[i] if isinstance(s, int) and s == 0 else slot
        return remote(src, slot, ring_send.at[i, way, s], ring_recv.at[i, way, s], ring_peer[way])

    def arrival(i, way, s):
        slot = bufs[i].at[index(me, way, s)]
        return remote(slot, slot, ring_send.at[i, way, s - 1], ring_recv.at[i, way, s - 1], ring_peer[way])

    def mate_copy(i, way, s, base):
        slot = bufs[i].at[index(base, way, s)]
        src = srcs[i] if isinstance(s, int) and s == 0 else slot
        return remote(src, slot, par_send.at[i, way, s], par_recv.at[i, way, s], mate)

    halo = [
        remote(h_ref, win.at[1], halo_send.at[0], halo_recv.at[0], near),
        remote(h_ref, win.at[0], halo_send.at[1], halo_recv.at[1], ring_peer[0]),
    ]
    own = [pltpu.make_async_copy(srcs[i], bufs[i].at[me], own_sem.at[i]) for i in range(3)]
    own.append(pltpu.make_async_copy(h_ref, win.at[2], own_sem.at[3]))

    greet([{"ctx": lax.rem(me + d, n)} for d in (1, 2, n - 1, n - 2)])
    for i in range(3):
        for way in range(2):
            ring(i, way, 0).start()
    for i in range(3):
        mate_copy(i, 0, 0, me).start()
    for copy in own:
        copy.start()

    def middle(s):
        for i in range(3):
            for way in range(2):
                arrival(i, way, s).wait_recv()
                ring(i, way, s).start()
                mate_copy(i, way, s, me).start()

    loop(1, 3, middle)
    for copy in halo:
        copy.start()
    loop(3, 7, middle)
    for s in (7, 8):
        for i in range(3):
            for way in range(2):
                if s <= counts[way][i]:
                    arrival(i, way, s).wait_recv()
                    if s < counts[way][i]:
                        ring(i, way, s).start()
                    mate_copy(i, way, s, me).start()

    for copy in own:
        copy.wait()
    for copy in halo:
        copy.wait_send()
        copy.wait_recv()

    def settle(s):
        for i in range(3):
            for way in range(2):
                ring(i, way, s).wait_send()
                mate_copy(i, way, s, me).wait_send()
                mate_copy(i, way, s, partner).wait_recv()

    for i in range(3):
        for way in range(2):
            ring(i, way, 0).wait_send()
        mate_copy(i, 0, 0, me).wait_send()
        mate_copy(i, 0, 0, partner).wait_recv()
    loop(1, 7, settle)
    for s in (7, 8):
        for i in range(3):
            for way in range(2):
                if s <= counts[way][i]:
                    if s < counts[way][i]:
                        ring(i, way, s).wait_send()
                    mate_copy(i, way, s, me).wait_send()
                    mate_copy(i, way, s, partner).wait_recv()


def gather(uk, uv, stats, halo):
    sem = pltpu.SemaphoreType.DMA
    return pl.pallas_call(
        gather_kernel,
        out_shape=(
            jax.ShapeDtypeStruct((32,) + uk.shape, bf16),
            jax.ShapeDtypeStruct((32,) + uv.shape, bf16),
            jax.ShapeDtypeStruct((32,) + stats.shape, f32),
            jax.ShapeDtypeStruct((3,) + halo.shape, bf16),
        ),
        in_specs=[VMEM] * 4,
        out_specs=(VMEM,) * 4,
        scratch_shapes=[
            sem((4,)), sem((3, 2, 8)), sem((3, 2, 8)), sem((3, 2, 9)), sem((3, 2, 9)), sem((2,)), sem((2,)),
        ],
        compiler_params=pltpu.CompilerParams(collective_id=0, has_side_effects=True),
    )(uk, uv, stats, halo)


def dot_nt(a, b):
    return lax.dot_general(a, b, (((1,), (1,)), ((), ())), preferred_element_type=f32)


def dot_tn(a, b):
    return lax.dot_general(a, b, (((0,), (0,)), ((), ())), preferred_element_type=f32)


def dot_nn(a, b):
    return jnp.dot(a, b, preferred_element_type=f32)


def attend_kernel(
    pos_ref, logp_ref, win_ref, uk_ref, uv_ref, q_ref, qr_ref, og_ref, st_ref, mask_ref, doc_ref,
    dq_ref, dqr_ref, dwk_ref, dwv_ref, dl_ref, acc, lat_t, gscale,
):
    step = pl.program_id(0)
    latent = win_ref[:, :512]

    @pl.when(step == 0)
    def _():
        acc[...] = jnp.zeros_like(acc)
        lat_t[...] = latent.astype(f32).T.astype(bf16)
        sums = jnp.sum(jnp.sum(st_ref[...], axis=0), axis=1, keepdims=True)
        live_total, live_count = sums[0:1], sums[1:2]
        gap = npo_beta * (live_total / live_count - logp_ref[0])
        weight = 2.0 * (1.0 / (1.0 + jnp.exp(-gap))) * 4096.0 / live_count
        gscale[...] = weight * mask_ref[...]

    scale = 1.0 / math.sqrt(NOPE + ROPE)
    key_idx = lax.broadcasted_iota(jnp.int32, (384, 128), 0) - 256
    query_idx = lax.broadcasted_iota(jnp.int32, (384, 128), 1)
    allowed = win_ref[:, 640:768].astype(f32) == doc_ref[...]
    allowed = allowed & (key_idx <= query_idx) & (pos_ref[0] * 128 + key_idx >= 0)
    low_lane = lax.broadcasted_iota(jnp.int32, (128, 128), 1) < ROPE
    keys = dot_nn(latent, uk_ref[...]).astype(bf16)
    values = dot_nn(latent, uv_ref[...]).astype(bf16)
    key_rope = win_ref[:, 512:640]
    query_rope = qr_ref[...].astype(f32)
    scale_col = gscale[...]
    part_k, part_v, rope_q, rope_k = [], [], [], 0.0
    for p in range(2):
        cols = slice(p * 128, p * 128 + 128)
        qn = q_ref[:, cols]
        mine = low_lane if p == 0 else jnp.logical_not(low_lane)
        qr = jnp.where(mine, query_rope, 0.0).astype(bf16)
        kh, vh = keys[:, cols], values[:, cols]
        grad = (scale_col * og_ref[:, cols].astype(f32)).astype(bf16)
        scores = dot_nt(kh, qn) + dot_nt(key_rope, qr)
        scores = jnp.where(allowed, scores * scale, -1e30)
        top = jnp.max(scores, axis=0, keepdims=True)
        expon = jnp.where(allowed, jnp.exp(scores - top), 0.0)
        probs = expon * (1.0 / jnp.sum(expon, axis=0, keepdims=True))
        low = probs.astype(bf16)
        dprob = dot_nt(vh, grad)
        delta = jnp.sum(low.astype(f32) * dprob, axis=0, keepdims=True)
        dscore = (probs * (dprob - delta) * scale).astype(bf16)
        dq_ref[:, cols] = dot_tn(dscore, kh).astype(bf16)
        rope_q.append(dot_tn(dscore, key_rope))
        rope_k = rope_k + dot_nn(dscore, qr)
        part_k.append(dot_nn(dscore, qn).astype(bf16))
        part_v.append(dot_nn(low, grad).astype(bf16))
    dqr_ref[...] = jnp.where(low_lane, rope_q[0], rope_q[1]).astype(bf16)
    part_k = jnp.concatenate(part_k, axis=1)
    part_v = jnp.concatenate(part_v, axis=1)
    acc[:, :512] += dot_nt(part_k, uk_ref[...]) + dot_nt(part_v, uv_ref[...])
    acc[:, 512:] += rope_k
    dwk_ref[...] = dot_nn(lat_t[...], part_k).astype(bf16)
    dwv_ref[...] = dot_nn(lat_t[...], part_v).astype(bf16)

    @pl.when(step == pl.num_programs(0) - 1)
    def _():
        dl_ref[...] = acc[...].astype(bf16)


def attend(position, ref_logp, window, uk, uv, q_nope, q_rope, out_grad, stats, mask_col, doc_row):
    width = uk.shape[1]

    def cols(rows, block):
        return pl.BlockSpec((rows, block), lambda i: (0, i))

    def whole(shape):
        return pl.BlockSpec(shape, lambda i: (0,) * len(shape))

    scalar = pl.BlockSpec(memory_space=pltpu.SMEM)
    return pl.pallas_call(
        attend_kernel,
        grid=(width // 256,),
        out_shape=(
            jax.ShapeDtypeStruct(q_nope.shape, bf16),
            jax.ShapeDtypeStruct(q_rope.shape, bf16),
            jax.ShapeDtypeStruct((512, width), bf16),
            jax.ShapeDtypeStruct((512, width), bf16),
            jax.ShapeDtypeStruct((384, 640), bf16),
        ),
        in_specs=[
            scalar, scalar, whole((384, 768)), cols(512, 256), cols(512, 256), cols(128, 256),
            cols(128, 128), cols(128, 256), whole(stats.shape), whole((128, 1)), whole((1, 128)),
        ],
        out_specs=(cols(128, 256), cols(128, 128), cols(512, 256), cols(512, 256), whole((384, 640))),
        scratch_shapes=[
            pltpu.VMEM((384, 640), f32), pltpu.VMEM((512, 384), bf16), pltpu.VMEM((128, 1), f32),
        ],
        compiler_params=pltpu.CompilerParams(dimension_semantics=("arbitrary",)),
    )(position, ref_logp, window, uk, uv, q_nope, q_rope, out_grad, stats, mask_col, doc_row)


def reduce_kernel(
    dwk, dwv, dl, ok, ov, olat, orope, par_buf, recv_buf, send_buf, back, mix, inbox, mine, final,
    par_send, par_recv, ring_send, ring_recv, back_send, back_recv, mix_send, mix_recv, all_send, all_recv,
):
    me, col = lax.axis_index("ctx"), lax.axis_index("dp")
    n, m = 32, 16
    core = lax.rem(me, 2)
    partner = me + 1 - 2 * core
    ring_peer = ({"ctx": lax.rem(me + 2, n)}, {"ctx": lax.rem(me + n - 2, n)})
    mate = {"ctx": partner}
    grads, counts = (dwk, dwv), (RIGHT, LEFT)
    others = [lax.rem(col + k, m) for k in range(1, m)]

    def to_mate(i, d):
        src = grads[i].at[lax.rem(partner + 2 * d, n)]
        return remote(src, par_buf.at[i, d], par_send.at[i, d], par_recv.at[i, d], mate)

    def back_copy(d):
        peer = {"ctx": lax.rem(me + n - d, n)}
        return remote(dl.at[2 - d], back.at[d - 1], back_send.at[d - 1], back_recv.at[d - 1], peer)

    def mix_copy(k):
        return remote(
            mix.at[others[k - 1]], inbox.at[k - 1], mix_send.at[k - 1], mix_recv.at[k - 1],
            {"dp": others[k - 1]},
        )

    def all_copy(k):
        return remote(
            mine, final.at[k], all_send.at[k - 1], all_recv.at[k - 1], {"dp": others[k - 1]}
        )

    def ring(i, way, s):
        return remote(
            send_buf.at[i, way, s], recv_buf.at[i, way, s], ring_send.at[i, way, s],
            ring_recv.at[i, way, s], ring_peer[way],
        )

    def local(i, d):
        to_mate(i, d).wait_recv()
        total = grads[i][lax.rem(me + 2 * d, n)].astype(f32)
        return total + par_buf[i, d].astype(f32)

    greet(
        [{"ctx": lax.rem(me + d, n)} for d in (1, 2, n - 1, n - 2)] + [{"dp": k} for k in others]
    )
    order = (8, 7, 9, 6, 10, 5, 11, 4, 12, 3, 13, 2, 14, 1, 15, 0)
    for d in order[:3]:
        for i in range(2):
            to_mate(i, d).start()
    for d in (2, 1):
        back_copy(d).start()
    for d in order[3:]:
        for i in range(2):
            to_mate(i, d).start()

    def ring_step(i, way, s):
        count = counts[way][i]
        d = count - s if way == 0 else 16 - count + s
        total = local(i, d)
        if not (isinstance(s, int) and s == 0):
            ring(i, way, s - 1).wait_recv()
            total = total + recv_buf[i, way, s - 1].astype(f32)
        send_buf[i, way, s] = total.astype(bf16)
        ring(i, way, s).start()

    def middle(s):
        for i in range(2):
            for way in range(2):
                ring_step(i, way, s)

    middle(0)
    for d in (2, 1):
        back_copy(d).wait_recv()
    summed = dl[2].astype(f32) + back[0].astype(f32) + back[1].astype(f32)
    mix[...] = summed.reshape(16, 8, 640).astype(bf16)
    for k in range(1, m):
        mix_copy(k).start()
    loop(1, 3, middle)
    total = mix[col].astype(f32)
    for k in range(1, m):
        mix_copy(k).wait_recv()
        total = total + inbox[k - 1].astype(f32)
    rope = total[:, 512:]
    rope = rope + pltpu.roll(rope, 64, 1)
    mine[...] = jnp.concatenate([total[:, :512], rope], axis=1).astype(bf16)
    for k in range(1, m):
        all_copy(k).start()
    loop(3, 7, middle)
    for i in range(2):
        for way in range(2):
            if counts[way][i] == 8:
                ring_step(i, way, 7)
    final[0] = mine[...]
    for k in range(1, m):
        all_copy(k).wait_recv()
    for j in range(m):
        rows = final[lax.rem(col + m - j, m)].astype(f32)
        olat[8 * j:8 * j + 8, :] = rows[:, :512].astype(bf16)
        orope[8 * j:8 * j + 8, :] = rows[:, 512:512 + ROPE].astype(bf16)
    outs = (ok, ov)
    for i in range(2):
        total = local(i, 0)
        for way in range(2):
            last = counts[way][i] - 1
            ring(i, way, last).wait_recv()
            total = total + recv_buf[i, way, last].astype(f32)
        outs[i][...] = total
    for i in range(2):
        for d in range(16):
            to_mate(i, d).wait_send()
        for way in range(2):
            for s in range(counts[way][i]):
                ring(i, way, s).wait_send()
    for d in (2, 1):
        back_copy(d).wait_send()
    for k in range(1, m):
        mix_copy(k).wait_send()
        all_copy(k).wait_send()


def reduce(dwk, dwv, dl):
    sem = pltpu.SemaphoreType.DMA
    width = dwk.shape[2]
    return pl.pallas_call(
        reduce_kernel,
        out_shape=(
            jax.ShapeDtypeStruct((16, width), f32),
            jax.ShapeDtypeStruct((16, width), f32),
            jax.ShapeDtypeStruct((128, 512), bf16),
            jax.ShapeDtypeStruct((128, ROPE), bf16),
        ),
        in_specs=[VMEM] * 3,
        out_specs=(VMEM,) * 4,
        scratch_shapes=[
            pltpu.VMEM((2, 16, 16, width), bf16),
            pltpu.VMEM((2, 2, 8, 16, width), bf16),
            pltpu.VMEM((2, 2, 8, 16, width), bf16),
            pltpu.VMEM((2, 128, 640), bf16),
            pltpu.VMEM((16, 8, 640), bf16),
            pltpu.VMEM((15, 8, 640), bf16),
            pltpu.VMEM((8, 640), bf16),
            pltpu.VMEM((16, 8, 640), bf16),
            sem((2, 16)), sem((2, 16)), sem((2, 2, 8)), sem((2, 2, 8)),
            sem((2,)), sem((2,)), sem((15,)), sem((15,)), sem((15,)), sem((15,)),
        ],
        compiler_params=pltpu.CompilerParams(collective_id=1, has_side_effects=True),
    )(dwk, dwv, dl)


def on_device(
    q_nope, q_rope, latent, k_rope, w_uk, w_uv, out_grad, log_prob, ref_logp, doc_ids, loss_mask
):
    mask_f = loss_mask.astype(f32)
    stats = jnp.concatenate(
        [(mask_f * log_prob)[None, :], mask_f[None, :], jnp.zeros((6, 128), f32)], axis=0
    )
    docs = jnp.broadcast_to(doc_ids.astype(bf16)[:, None], (128, 128))
    halo = jnp.concatenate([latent, k_rope, k_rope, docs], axis=1)
    position = lax.axis_index("ctx").astype(jnp.int32).reshape(1)
    full_uk, full_uv, all_stats, window = gather(w_uk, w_uv, stats, halo)
    width = w_uk.shape[1]
    dq_nope, dq_rope, dwk, dwv, dl = attend(
        position, ref_logp, window.reshape(384, 768), full_uk.reshape(512, width),
        full_uv.reshape(512, width), q_nope, q_rope, out_grad, all_stats, mask_f[:, None],
        doc_ids.astype(f32)[None, :],
    )
    dw_uk, dw_uv, d_latent, d_krope = reduce(
        dwk.reshape(32, 16, width), dwv.reshape(32, 16, width), dl.reshape(3, 128, 640)
    )
    return dq_nope, dq_rope, d_latent, d_krope, dw_uk, dw_uv


def solution(mesh):
    both, rows, flat = P("ctx", "dp"), P("ctx", None), P("ctx")
    return jax.shard_map(
        on_device,
        mesh=mesh,
        in_specs=(both, both, rows, rows, both, both, both, flat, P(), flat, flat),
        out_specs=(both, both, rows, rows, both, both),
        check_vma=False,
    )
```

```python
import math

import jax
import jax.numpy as jnp
from jax import lax
from jax.experimental import pallas as pl
from jax.experimental.pallas import tpu as pltpu
from jax.sharding import PartitionSpec as P

NOPE = 128
ROPE = 64
npo_beta = 1.0
MESH = pl.DeviceIdType.MESH
VMEM = pl.BlockSpec(memory_space=pltpu.VMEM)
f32 = jnp.float32
bf16 = jnp.bfloat16


def greet(peers):
    barrier = pltpu.get_barrier_semaphore()
    for peer in peers:
        pl.semaphore_signal(barrier, inc=1, device_id=peer, device_id_type=MESH)
    pl.semaphore_wait(barrier, len(peers))


def remote(src, dst, send, recv, peer):
    return pltpu.make_async_remote_copy(
        src_ref=src, dst_ref=dst, send_sem=send, recv_sem=recv, device_id=peer, device_id_type=MESH
    )


def relay(d):
    return 3 * ((d - 1) // 3)


def gather_kernel(
    uk_ref, uv_ref, lat_ref, rope_ref, logp_ref, base_ref, doc_ref, mask_ref,
    buk, buv, bst, win, win_r, tile,
    own_sem, ring_send, ring_recv, par_send, par_recv, halo_send, halo_recv,
):
    me = lax.axis_index("ctx")
    n = 32
    core = lax.rem(me, 2)
    partner = me + 1 - 2 * core
    mate = {"ctx": partner}
    srcs, bufs = (uk_ref, uv_ref, tile), (buk, buv, bst)
    counts = ((7, 7, 8), (8, 8, 7))

    mask = mask_ref[...].astype(f32)
    tile[0:1, :] = mask * logp_ref[...]
    tile[1:2, :] = mask
    tile[2:3, :] = doc_ref[...].astype(f32)
    tile[3:4, :] = jnp.broadcast_to(base_ref[...], (1, 128))
    tile[4:8, :] = jnp.zeros((4, 128), f32)

    def away(way, hops):
        return lax.rem(me + 2 * hops, n) if way == 0 else lax.rem(me + n - 2 * hops, n)

    def origin(base, way, d):
        return lax.rem(base + n - 2 * d, n) if way == 0 else lax.rem(base + 2 * d, n)

    def send(i, way, d):
        slot = bufs[i].at[origin(me, way, relay(d))]
        src = srcs[i] if relay(d) == 0 else slot
        peer = {"ctx": away(way, d - relay(d))}
        return remote(src, slot, ring_send.at[i, way, d], ring_recv.at[i, way, d], peer)

    def arrival(i, way, d):
        slot = bufs[i].at[origin(me, way, d)]
        peer = {"ctx": away(1 - way, d - relay(d))}
        return remote(slot, slot, ring_send.at[i, way, d], ring_recv.at[i, way, d], peer)

    def mate_copy(i, way, d, base):
        slot = bufs[i].at[origin(base, way, d)]
        src = srcs[i] if d == 0 else slot
        return remote(src, slot, par_send.at[i, way, d], par_recv.at[i, way, d], mate)

    next_chip = {"ctx": away(0, 1)}
    halo = [
        remote(lat_ref, win.at[0], halo_send.at[0], halo_recv.at[0], next_chip),
        remote(rope_ref, win_r.at[0], halo_send.at[1], halo_recv.at[1], next_chip),
    ]
    give = 2 - 2 * core
    halo_mate = [
        remote(win.at[give], win.at[1], halo_send.at[2], halo_recv.at[2], mate),
        remote(win_r.at[give], win_r.at[1], halo_send.at[3], halo_recv.at[3], mate),
    ]
    flows = [(i, way) for i in range(3) for way in range(2)]

    def some(d):
        return [(i, way) for i, way in flows if d <= counts[way][i]]

    greet([{"ctx": lax.rem(me + d, n)} for d in (1, 2, 4, 6, n - 1, n - 2, n - 4, n - 6)])
    for d in (3, 2, 1):
        for i, way in flows:
            send(i, way, d).start()
    own = [pltpu.make_async_copy(srcs[i], bufs[i].at[me], own_sem.at[i]) for i in range(3)]
    own.append(pltpu.make_async_copy(lat_ref, win.at[2], own_sem.at[3]))
    own.append(pltpu.make_async_copy(rope_ref, win_r.at[2], own_sem.at[4]))
    for copy in own + halo:
        copy.start()
    for i in range(3):
        mate_copy(i, 0, 0, me).start()
    for i, way in flows:
        arrival(i, way, 3).wait_recv()
        for d in (6, 5, 4):
            send(i, way, d).start()
    for d in (1, 2):
        for i, way in flows:
            arrival(i, way, d).wait_recv()
    for i, way in flows:
        for d in (1, 2, 3):
            mate_copy(i, way, d, me).start()
    for i, way in flows:
        arrival(i, way, 6).wait_recv()
        for d in (8, 7):
            if d <= counts[way][i]:
                send(i, way, d).start()
    for copy in own:
        copy.wait()
    for copy in halo:
        copy.wait_recv()
    for copy in halo_mate:
        copy.start()
    for d in (4, 5):
        for i, way in flows:
            arrival(i, way, d).wait_recv()
    for i, way in flows:
        for d in (4, 5, 6):
            mate_copy(i, way, d, me).start()
    for d in (7, 8):
        for i, way in some(d):
            arrival(i, way, d).wait_recv()
            mate_copy(i, way, d, me).start()
    for i in range(3):
        mate_copy(i, 0, 0, me).wait_send()
        mate_copy(i, 0, 0, partner).wait_recv()
    for d in range(1, 9):
        for i, way in some(d):
            send(i, way, d).wait_send()
            mate_copy(i, way, d, me).wait_send()
            mate_copy(i, way, d, partner).wait_recv()
    for copy in halo:
        copy.wait_send()
    for copy in halo_mate:
        copy.wait_send()
        copy.wait_recv()


def gather(uk, uv, latent, rope, logp, base, docs, mask):
    sem = pltpu.SemaphoreType.DMA
    return pl.pallas_call(
        gather_kernel,
        out_shape=(
            jax.ShapeDtypeStruct((32,) + uk.shape, bf16),
            jax.ShapeDtypeStruct((32,) + uv.shape, bf16),
            jax.ShapeDtypeStruct((32, 8, 128), f32),
            jax.ShapeDtypeStruct((3,) + latent.shape, bf16),
            jax.ShapeDtypeStruct((3,) + rope.shape, bf16),
        ),
        in_specs=[VMEM] * 8,
        out_specs=(VMEM,) * 5,
        scratch_shapes=[
            pltpu.VMEM((8, 128), f32),
            sem((5,)), sem((3, 2, 9)), sem((3, 2, 9)), sem((3, 2, 9)), sem((3, 2, 9)), sem((4,)), sem((4,)),
        ],
        compiler_params=pltpu.CompilerParams(collective_id=0, has_side_effects=True),
    )(uk, uv, latent, rope, logp, base, docs, mask)


def dot_nt(a, b):
    return lax.dot_general(a, b, (((1,), (1,)), ((), ())), preferred_element_type=f32)


def dot_tn(a, b):
    return lax.dot_general(a, b, (((0,), (0,)), ((), ())), preferred_element_type=f32)


def dot_nn(a, b):
    return jnp.dot(a, b, preferred_element_type=f32)


def attend_kernel(
    win_ref, rope_ref, uk_ref, uv_ref, q_ref, qr_ref, og_ref, st_ref,
    dq_ref, dqr_ref, dwk_ref, dwv_ref, dl_ref, acc, lat_t, gscale, rope_k_ref, docs,
):
    step = pl.program_id(0)
    me = lax.axis_index("ctx")
    latent = win_ref[...]

    @pl.when(step == 0)
    def _():
        acc[...] = jnp.zeros_like(acc)
        lat_t[...] = latent.astype(f32).T.astype(bf16)
        sums = jnp.sum(jnp.sum(st_ref[...], axis=0), axis=1, keepdims=True)
        live_total, live_count = sums[0:1], sums[1:2]
        own = st_ref[me]
        gap = npo_beta * (live_total / live_count - own[3:4])
        weight = 2.0 * (1.0 / (1.0 + jnp.exp(-gap))) * 4096.0 / live_count
        gscale[...] = jnp.broadcast_to(weight * own[1:2], (128, 128)).T
        for t in range(3):
            rows = slice(t * 128, t * 128 + 128)
            there = st_ref[lax.rem(me + 30 + t, 32)]
            docs[rows, :] = jnp.broadcast_to(there[2:3], (128, 128)).T
            column = rope_ref[t].astype(f32).T
            rope_k_ref[rows, :] = jnp.concatenate([column, column], axis=1).astype(bf16)

    scale = 1.0 / math.sqrt(NOPE + ROPE)
    key_idx = lax.broadcasted_iota(jnp.int32, (384, 128), 0) - 256
    query_idx = lax.broadcasted_iota(jnp.int32, (384, 128), 1)
    allowed = docs[...] == st_ref[me][2:3]
    allowed = allowed & (key_idx <= query_idx) & (me * 128 + key_idx >= 0)
    low_lane = lax.broadcasted_iota(jnp.int32, (128, 128), 1) < ROPE
    keys = dot_nn(latent, uk_ref[...]).astype(bf16)
    values = dot_nn(latent, uv_ref[...]).astype(bf16)
    key_rope = rope_k_ref[...]
    query_rope = qr_ref[...].astype(f32)
    scale_col = gscale[...]
    part_k, part_v, rope_q, rope_k = [], [], [], 0.0
    for p in range(2):
        cols = slice(p * 128, p * 128 + 128)
        qn = q_ref[:, cols]
        mine = low_lane if p == 0 else jnp.logical_not(low_lane)
        qr = jnp.where(mine, query_rope, 0.0).astype(bf16)
        kh, vh = keys[:, cols], values[:, cols]
        grad = (scale_col * og_ref[:, cols].astype(f32)).astype(bf16)
        scores = dot_nt(kh, qn) + dot_nt(key_rope, qr)
        scores = jnp.where(allowed, scores * scale, -1e30)
        top = jnp.max(scores, axis=0, keepdims=True)
        expon = jnp.where(allowed, jnp.exp(scores - top), 0.0)
        probs = expon * (1.0 / jnp.sum(expon, axis=0, keepdims=True))
        low = probs.astype(bf16)
        dprob = dot_nt(vh, grad)
        delta = jnp.sum(low.astype(f32) * dprob, axis=0, keepdims=True)
        dscore = (probs * (dprob - delta) * scale).astype(bf16)
        dq_ref[:, cols] = dot_tn(dscore, kh).astype(bf16)
        rope_q.append(dot_tn(dscore, key_rope))
        rope_k = rope_k + dot_nn(dscore, qr)
        part_k.append(dot_nn(dscore, qn).astype(bf16))
        part_v.append(dot_nn(low, grad).astype(bf16))
    dqr_ref[...] = jnp.where(low_lane, rope_q[0], rope_q[1]).astype(bf16)
    part_k = jnp.concatenate(part_k, axis=1)
    part_v = jnp.concatenate(part_v, axis=1)
    acc[:, :512] += dot_nt(part_k, uk_ref[...]) + dot_nt(part_v, uv_ref[...])
    acc[:, 512:] += rope_k
    dwk_ref[...] = dot_nn(lat_t[...], part_k).astype(bf16)
    dwv_ref[...] = dot_nn(lat_t[...], part_v).astype(bf16)

    @pl.when(step == pl.num_programs(0) - 1)
    def _():
        for t in range(3):
            dl_ref[:, t] = acc[t * 128:t * 128 + 128, :].reshape(16, 8, 640).astype(bf16)


def attend(window, rope, uk, uv, q_nope, q_rope, out_grad, stats):
    width = uk.shape[1]

    def cols(rows, block):
        return pl.BlockSpec((rows, block), lambda i: (0, i))

    def whole(shape):
        return pl.BlockSpec(shape, lambda i: (0,) * len(shape))

    return pl.pallas_call(
        attend_kernel,
        grid=(width // 256,),
        out_shape=(
            jax.ShapeDtypeStruct(q_nope.shape, bf16),
            jax.ShapeDtypeStruct(q_rope.shape, bf16),
            jax.ShapeDtypeStruct((512, width), bf16),
            jax.ShapeDtypeStruct((512, width), bf16),
            jax.ShapeDtypeStruct((16, 3, 8, 640), bf16),
        ),
        in_specs=[
            whole((384, 512)), whole((3, 64, 128)), cols(512, 256), cols(512, 256), cols(128, 256),
            cols(128, 128), cols(128, 256), whole(stats.shape),
        ],
        out_specs=(cols(128, 256), cols(128, 128), cols(512, 256), cols(512, 256), whole((16, 3, 8, 640))),
        scratch_shapes=[
            pltpu.VMEM((384, 640), f32), pltpu.VMEM((512, 384), bf16), pltpu.VMEM((128, 128), f32),
            pltpu.VMEM((384, 128), bf16), pltpu.VMEM((384, 128), f32),
        ],
        compiler_params=pltpu.CompilerParams(dimension_semantics=("arbitrary",)),
    )(window, rope, uk, uv, q_nope, q_rope, out_grad, stats)


def reduce_kernel(
    dwk, dwv, dl, ok, ov, final, par_buf, recv_buf, send_buf, inbox, halves, back, mine,
    par_send, par_recv, ring_send, ring_recv, back_send, back_recv, mix_send, mix_recv, all_send, all_recv,
):
    me, col = lax.axis_index("ctx"), lax.axis_index("dp")
    n, m = 32, 16
    core = lax.rem(me, 2)
    partner = me + 1 - 2 * core
    mate = {"ctx": partner}
    grads, counts = (dwk, dwv), ((8, 7), (7, 8))
    others = [lax.rem(col + k, m) for k in range(1, m)]
    flows = [(i, way) for i in range(2) for way in range(2)]

    def away(way, hops):
        return lax.rem(me + 2 * hops, n) if way == 0 else lax.rem(me + n - 2 * hops, n)

    def to_mate(i, d):
        src = grads[i].at[lax.rem(partner + 2 * d, n)]
        return remote(src, par_buf.at[i, d], par_send.at[i, d], par_recv.at[i, d], mate)

    def mix_copy(k):
        return remote(
            dl.at[others[k - 1]], inbox.at[k - 1], mix_send.at[k - 1], mix_recv.at[k - 1],
            {"dp": others[k - 1]},
        )

    def back_copy(d):
        peer = {"ctx": lax.rem(me + n - d, n)}
        return remote(halves.at[d - 1], back.at[d - 1], back_send.at[d - 1], back_recv.at[d - 1], peer)

    def all_copy(k):
        return remote(mine, final.at[k], all_send.at[k - 1], all_recv.at[k - 1], {"dp": others[k - 1]})

    def ring(i, way, d):
        peer = {"ctx": away(way, d - relay(d))}
        return remote(
            send_buf.at[i, way, d], recv_buf.at[i, way, d], ring_send.at[i, way, d],
            ring_recv.at[i, way, d], peer,
        )

    def local(i, d):
        to_mate(i, d).wait_recv()
        total = grads[i][lax.rem(me + 2 * d, n)].astype(f32)
        return total + par_buf[i, d].astype(f32)

    def arrived(i, way, first, last):
        total = 0.0
        for d in range(first, min(last, counts[way][i]) + 1):
            ring(i, way, d).wait_recv()
            total = total + recv_buf[i, way, d].astype(f32)
        return total

    def pass_on(i, way, d):
        total = local(i, d if way == 0 else 16 - d)
        if d in (3, 6):
            total = total + arrived(i, way, d + 1, d + 3)
        send_buf[i, way, d] = total.astype(bf16)
        ring(i, way, d).start()

    greet(
        [{"ctx": lax.rem(me + d, n)} for d in (1, 2, 4, 6, n - 1, n - 2, n - 4, n - 6)]
        + [{"dp": k} for k in others]
    )
    order = (8, 7, 9, 5, 11, 4, 12, 2, 14, 1, 15, 6, 10, 3, 13, 0)
    for d in order[:3]:
        for i in range(2):
            to_mate(i, d).start()
    for k in range(1, m):
        mix_copy(k).start()
    for d in order[3:]:
        for i in range(2):
            to_mate(i, d).start()
    for d in (8, 7, 5, 4):
        for i, way in flows:
            if d <= counts[way][i]:
                pass_on(i, way, d)
    for i, way in flows:
        pass_on(i, way, 6)
    total = dl[col].astype(f32)
    for k in range(1, m):
        mix_copy(k).wait_recv()
        total = total + inbox[k - 1].astype(f32)
    halves[0] = total[1].astype(bf16)
    halves[1] = total[0].astype(bf16)
    for d in (2, 1):
        back_copy(d).start()
    for d in (2, 1):
        for i, way in flows:
            pass_on(i, way, d)
    for i, way in flows:
        pass_on(i, way, 3)
    total = total[2]
    for d in (2, 1):
        back_copy(d).wait_recv()
        total = total + back[d - 1].astype(f32)
    rope = total[:, 512:]
    rope = rope + pltpu.roll(rope, 64, 1)
    rows = jnp.concatenate([total[:, :512], rope], axis=1).astype(bf16)
    mine[...] = rows
    final[0] = rows
    for k in range(1, m):
        all_copy(k).start()
    outs = (ok, ov)
    for i in range(2):
        outs[i][...] = local(i, 0) + arrived(i, 0, 1, 3) + arrived(i, 1, 1, 3)
    for k in range(1, m):
        all_copy(k).wait_recv()
    for i in range(2):
        for d in range(16):
            to_mate(i, d).wait_send()
        for way in range(2):
            for d in range(1, counts[way][i] + 1):
                ring(i, way, d).wait_send()
    for d in (2, 1):
        back_copy(d).wait_send()
    for k in range(1, m):
        mix_copy(k).wait_send()
        all_copy(k).wait_send()


def reduce(dwk, dwv, dl):
    sem = pltpu.SemaphoreType.DMA
    width = dwk.shape[2]
    return pl.pallas_call(
        reduce_kernel,
        out_shape=(
            jax.ShapeDtypeStruct((16, width), f32),
            jax.ShapeDtypeStruct((16, width), f32),
            jax.ShapeDtypeStruct((16, 8, 640), bf16),
        ),
        in_specs=[VMEM] * 3,
        out_specs=(VMEM,) * 3,
        scratch_shapes=[
            pltpu.VMEM((2, 16, 16, width), bf16),
            pltpu.VMEM((2, 2, 9, 16, width), bf16),
            pltpu.VMEM((2, 2, 9, 16, width), bf16),
            pltpu.VMEM((15, 3, 8, 640), bf16),
            pltpu.VMEM((2, 8, 640), bf16),
            pltpu.VMEM((2, 8, 640), bf16),
            pltpu.VMEM((8, 640), bf16),
            sem((2, 16)), sem((2, 16)), sem((2, 2, 9)), sem((2, 2, 9)),
            sem((2,)), sem((2,)), sem((15,)), sem((15,)), sem((15,)), sem((15,)),
        ],
        compiler_params=pltpu.CompilerParams(collective_id=1, has_side_effects=True),
    )(dwk, dwv, dl)


def place_kernel(wk_ref, wv_ref, rows_ref, ok, ov, olat, orope):
    col = lax.axis_index("dp")
    ok[...] = wk_ref[...]
    ov[...] = wv_ref[...]
    pieces = [rows_ref[lax.rem(col + 16 - j, 16)].astype(f32) for j in range(16)]
    rows = jnp.concatenate(pieces, axis=0)
    olat[...] = rows[:, :512].astype(bf16)
    orope[...] = rows[:, 512:].T[:ROPE].astype(bf16)


def place(wk, wv, rows):
    return pl.pallas_call(
        place_kernel,
        out_shape=(
            jax.ShapeDtypeStruct(wk.shape, f32),
            jax.ShapeDtypeStruct(wv.shape, f32),
            jax.ShapeDtypeStruct((128, 512), bf16),
            jax.ShapeDtypeStruct((ROPE, 128), bf16),
        ),
        in_specs=[VMEM] * 3,
        out_specs=(VMEM,) * 4,
    )(wk, wv, rows)


def on_device(
    q_nope, q_rope, latent, k_rope, w_uk, w_uv, out_grad, log_prob, ref_logp, doc_ids, loss_mask
):
    full_uk, full_uv, stats, window, rope = gather(
        w_uk, w_uv, latent, k_rope.T, log_prob[None, :], ref_logp[None, :], doc_ids[None, :],
        loss_mask[None, :],
    )
    width = w_uk.shape[1]
    dq_nope, dq_rope, dwk, dwv, dl = attend(
        window.reshape(384, 512), rope, full_uk.reshape(512, width),
        full_uv.reshape(512, width), q_nope, q_rope, out_grad, stats,
    )
    dw_uk, dw_uv, d_latent, d_krope = place(
        *reduce(dwk.reshape(32, 16, width), dwv.reshape(32, 16, width), dl)
    )
    return dq_nope, dq_rope, d_latent, d_krope.T, dw_uk, dw_uv


def solution(mesh):
    both, rows, flat = P("ctx", "dp"), P("ctx", None), P("ctx")
    return jax.shard_map(
        on_device,
        mesh=mesh,
        in_specs=(both, both, rows, rows, both, both, both, flat, P(), flat, flat),
        out_specs=(both, both, rows, rows, both, both),
        check_vma=False,
    )
```

```python
import math

import jax
import jax.numpy as jnp
from jax import lax
from jax.experimental import pallas as pl
from jax.experimental.pallas import tpu as pltpu
from jax.sharding import PartitionSpec as P

NOPE = 128
ROPE = 64
npo_beta = 1.0
MESH = pl.DeviceIdType.MESH
VMEM = pl.BlockSpec(memory_space=pltpu.VMEM)
f32 = jnp.float32
bf16 = jnp.bfloat16


def greet(peers):
    barrier = pltpu.get_barrier_semaphore()
    for peer in peers:
        pl.semaphore_signal(barrier, inc=1, device_id=peer, device_id_type=MESH)
    pl.semaphore_wait(barrier, len(peers))


def remote(src, dst, send, recv, peer):
    return pltpu.make_async_remote_copy(
        src_ref=src, dst_ref=dst, send_sem=send, recv_sem=recv, device_id=peer, device_id_type=MESH
    )


def relay(d):
    return 3 * ((d - 1) // 3)


def gather_kernel(
    uk_ref, uv_ref, lat_ref, rope_ref, logp_ref, doc_ref, mask_ref,
    buf, win, item, near,
    own_sem, ring_send, ring_recv, par_send, par_recv, halo_send, halo_recv,
):
    me = lax.axis_index("ctx")
    n = 32
    core = lax.rem(me, 2)
    partner = me + 1 - 2 * core
    mate = {"ctx": partner}
    counts = (7, 8)
    width = uk_ref.shape[1]

    item[:, :width] = uk_ref[...]
    item[:, width:2 * width] = uv_ref[...]
    mask = mask_ref[...].astype(f32)
    masked = mask * logp_ref[...]
    high = masked.astype(bf16).astype(f32)
    rest = masked - high
    middle = rest.astype(bf16).astype(f32)
    small = [doc_ref[...].astype(f32), mask, high, middle, rest - middle, jnp.zeros((11, 128), f32)]
    item[:, 2 * width:] = jnp.concatenate(small, axis=0).astype(bf16)
    near[:, :512] = lat_ref[...]
    column = rope_ref[...].astype(f32).T
    near[:, 512:] = jnp.concatenate([column, column], axis=1).astype(bf16)

    def away(way, hops):
        return lax.rem(me + 2 * hops, n) if way == 0 else lax.rem(me + n - 2 * hops, n)

    def origin(base, way, d):
        return lax.rem(base + n - 2 * d, n) if way == 0 else lax.rem(base + 2 * d, n)

    def send(way, d):
        slot = buf.at[origin(me, way, relay(d))]
        src = item if relay(d) == 0 else slot
        peer = {"ctx": away(way, d - relay(d))}
        return remote(src, slot, ring_send.at[way, d], ring_recv.at[way, d], peer)

    def arrival(way, d):
        slot = buf.at[origin(me, way, d)]
        peer = {"ctx": away(1 - way, d - relay(d))}
        return remote(slot, slot, ring_send.at[way, d], ring_recv.at[way, d], peer)

    def mate_copy(way, d, base):
        slot = buf.at[origin(base, way, d)]
        src = item if d == 0 else slot
        return remote(src, slot, par_send.at[way, d], par_recv.at[way, d], mate)

    halo = remote(near, win.at[0], halo_send.at[0], halo_recv.at[0], {"ctx": away(0, 1)})
    halo_mate = remote(win.at[2 - 2 * core], win.at[1], halo_send.at[1], halo_recv.at[1], mate)
    ways = (1, 0)

    greet([{"ctx": lax.rem(me + d, n)} for d in (1, 2, 4, 6, n - 1, n - 2, n - 4, n - 6)])
    for d in (3, 2, 1):
        for way in ways:
            send(way, d).start()
    own = [
        pltpu.make_async_copy(item, buf.at[me], own_sem.at[0]),
        pltpu.make_async_copy(near, win.at[2], own_sem.at[1]),
    ]
    for copy in own:
        copy.start()
    mate_copy(0, 0, me).start()
    halo.start()
    for way in ways:
        arrival(way, 3).wait_recv()
        for d in (6, 5, 4):
            send(way, d).start()
    for d in (1, 2):
        for way in ways:
            arrival(way, d).wait_recv()
    for d in (1, 2, 3):
        for way in ways:
            mate_copy(way, d, me).start()
    for way in ways:
        arrival(way, 6).wait_recv()
        for d in (8, 7):
            if d <= counts[way]:
                send(way, d).start()
    for copy in own:
        copy.wait()
    halo.wait_recv()
    halo_mate.start()
    for d in (4, 5):
        for way in ways:
            arrival(way, d).wait_recv()
    for d in (4, 5, 6):
        for way in ways:
            mate_copy(way, d, me).start()
    for d in (7, 8):
        for way in ways:
            if d <= counts[way]:
                arrival(way, d).wait_recv()
                mate_copy(way, d, me).start()
    mate_copy(0, 0, me).wait_send()
    mate_copy(0, 0, partner).wait_recv()
    for d in range(1, 9):
        for way in ways:
            if d <= counts[way]:
                send(way, d).wait_send()
                mate_copy(way, d, me).wait_send()
                mate_copy(way, d, partner).wait_recv()
    halo.wait_send()
    halo_mate.wait_send()
    halo_mate.wait_recv()


def gather(uk, uv, latent, rope, logp, docs, mask):
    sem = pltpu.SemaphoreType.DMA
    total = 2 * uk.shape[1] + 128
    return pl.pallas_call(
        gather_kernel,
        out_shape=(
            jax.ShapeDtypeStruct((32, 16, total), bf16),
            jax.ShapeDtypeStruct((3, 128, 640), bf16),
        ),
        in_specs=[VMEM] * 7,
        out_specs=(VMEM,) * 2,
        scratch_shapes=[
            pltpu.VMEM((16, total), bf16),
            pltpu.VMEM((128, 640), bf16),
            sem((2,)), sem((2, 9)), sem((2, 9)), sem((2, 9)), sem((2, 9)), sem((2,)), sem((2,)),
        ],
        compiler_params=pltpu.CompilerParams(collective_id=0, has_side_effects=True),
    )(uk, uv, latent, rope, logp, docs, mask)


def dot_nt(a, b):
    return lax.dot_general(a, b, (((1,), (1,)), ((), ())), preferred_element_type=f32)


def dot_tn(a, b):
    return lax.dot_general(a, b, (((0,), (0,)), ((), ())), preferred_element_type=f32)


def dot_nn(a, b):
    return jnp.dot(a, b, preferred_element_type=f32)


def small_rows(st_ref, idx):
    return st_ref[pl.ds(pl.multiple_of(idx * 16, 16), 16), :].astype(f32)


def attend_kernel(
    win_ref, uk_ref, uv_ref, q_ref, qr_ref, og_ref, st_ref, base_ref,
    dq_ref, dqr_ref, dw_ref, dl_ref, acc, lat_t, gscale, docs,
):
    step = pl.program_id(0)
    me = lax.axis_index("ctx")
    latent = win_ref[:, :512]

    @pl.when(step == 0)
    def _():
        acc[...] = jnp.zeros_like(acc)
        lat_t[...] = latent.astype(f32).T.astype(bf16)
        every = st_ref[...].astype(f32).reshape(32, 16, 128)
        sums = jnp.sum(jnp.sum(every, axis=0), axis=1, keepdims=True)
        live_count, live_total = sums[1:2], sums[2:3] + sums[3:4] + sums[4:5]
        own = small_rows(st_ref, me)
        gap = npo_beta * (live_total / live_count - base_ref[...])
        weight = 2.0 * (1.0 / (1.0 + jnp.exp(-gap))) * 4096.0 / live_count
        gscale[...] = jnp.broadcast_to(weight * own[1:2], (128, 128)).T
        for t in range(3):
            there = small_rows(st_ref, lax.rem(me + 30 + t, 32))
            docs[t * 128:t * 128 + 128, :] = jnp.broadcast_to(there[0:1], (128, 128)).T

    scale = 1.0 / math.sqrt(NOPE + ROPE)
    key_idx = lax.broadcasted_iota(jnp.int32, (384, 128), 0) - 256
    query_idx = lax.broadcasted_iota(jnp.int32, (384, 128), 1)
    allowed = docs[...] == small_rows(st_ref, me)[0:1]
    allowed = allowed & (key_idx <= query_idx) & (me * 128 + key_idx >= 0)
    low_lane = lax.broadcasted_iota(jnp.int32, (128, 128), 1) < ROPE
    keys = dot_nn(latent, uk_ref[...]).astype(bf16)
    values = dot_nn(latent, uv_ref[...]).astype(bf16)
    key_rope = win_ref[:, 512:]
    query_rope = qr_ref[...].astype(f32)
    scale_col = gscale[...]
    part_k, part_v, rope_q, rope_k = [], [], [], 0.0
    for p in range(2):
        cols = slice(p * 128, p * 128 + 128)
        qn = q_ref[:, cols]
        mine = low_lane if p == 0 else jnp.logical_not(low_lane)
        qr = jnp.where(mine, query_rope, 0.0).astype(bf16)
        kh, vh = keys[:, cols], values[:, cols]
        grad = (scale_col * og_ref[:, cols].astype(f32)).astype(bf16)
        scores = dot_nt(kh, qn) + dot_nt(key_rope, qr)
        scores = jnp.where(allowed, scores * scale, -1e30)
        top = jnp.max(scores, axis=0, keepdims=True)
        expon = jnp.where(allowed, jnp.exp(scores - top), 0.0)
        probs = expon * (1.0 / jnp.sum(expon, axis=0, keepdims=True))
        low = probs.astype(bf16)
        dprob = dot_nt(vh, grad)
        delta = jnp.sum(low.astype(f32) * dprob, axis=0, keepdims=True)
        dscore = (probs * (dprob - delta) * scale).astype(bf16)
        dq_ref[:, cols] = dot_tn(dscore, kh).astype(bf16)
        rope_q.append(dot_tn(dscore, key_rope))
        rope_k = rope_k + dot_nn(dscore, qr)
        part_k.append(dot_nn(dscore, qn).astype(bf16))
        part_v.append(dot_nn(low, grad).astype(bf16))
    dqr_ref[...] = jnp.where(low_lane, rope_q[0], rope_q[1]).astype(bf16)
    part_k = jnp.concatenate(part_k, axis=1)
    part_v = jnp.concatenate(part_v, axis=1)
    acc[:, :512] += dot_nt(part_k, uk_ref[...]) + dot_nt(part_v, uv_ref[...])
    acc[:, 512:] += rope_k
    half = pl.num_programs(0) * 256
    first = pl.multiple_of(step * 256, 256)
    dw_ref[:, pl.ds(first, 256)] = dot_nn(lat_t[...], part_k).astype(bf16)
    dw_ref[:, pl.ds(pl.multiple_of(half + first, 256), 256)] = dot_nn(lat_t[...], part_v).astype(bf16)

    @pl.when(step == pl.num_programs(0) - 1)
    def _():
        for t in range(3):
            dl_ref[:, t] = acc[t * 128:t * 128 + 128, :].reshape(16, 8, 640).astype(bf16)


def attend(window, full, q_nope, q_rope, out_grad, base):
    width = q_nope.shape[1]

    def cols(rows, block):
        return pl.BlockSpec((rows, block), lambda i: (0, i))

    def whole(shape):
        return pl.BlockSpec(shape, lambda i: (0,) * len(shape))

    return pl.pallas_call(
        attend_kernel,
        grid=(width // 256,),
        out_shape=(
            jax.ShapeDtypeStruct(q_nope.shape, bf16),
            jax.ShapeDtypeStruct(q_rope.shape, bf16),
            jax.ShapeDtypeStruct((512, 2 * width), bf16),
            jax.ShapeDtypeStruct((16, 3, 8, 640), bf16),
        ),
        in_specs=[
            whole((384, 640)), cols(512, 256), pl.BlockSpec((512, 256), lambda i: (0, i + width // 256)),
            cols(128, 256), cols(128, 128), cols(128, 256),
            pl.BlockSpec((512, 128), lambda i: (0, width // 64)), whole((1, 1)),
        ],
        out_specs=(cols(128, 256), cols(128, 128), whole((512, 2 * width)), whole((16, 3, 8, 640))),
        scratch_shapes=[
            pltpu.VMEM((384, 640), f32), pltpu.VMEM((512, 384), bf16), pltpu.VMEM((128, 128), f32),
            pltpu.VMEM((384, 128), f32),
        ],
        compiler_params=pltpu.CompilerParams(dimension_semantics=("arbitrary",)),
    )(window, full, full, q_nope, q_rope, out_grad, full, base)


def reduce_kernel(
    dw, dl, ok, ov, final, par_buf, recv_buf, send_buf, inbox, halves, back, mine,
    par_send, par_recv, ring_send, ring_recv, back_send, back_recv, mix_send, mix_recv, all_send, all_recv,
):
    me, col = lax.axis_index("ctx"), lax.axis_index("dp")
    n, m = 32, 16
    core = lax.rem(me, 2)
    partner = me + 1 - 2 * core
    mate = {"ctx": partner}
    counts = (8, 7)
    others = [lax.rem(col + k, m) for k in range(1, m)]
    width = ok.shape[1]

    def away(way, hops):
        return lax.rem(me + 2 * hops, n) if way == 0 else lax.rem(me + n - 2 * hops, n)

    def to_mate(d):
        src = dw.at[lax.rem(partner + 2 * d, n)]
        return remote(src, par_buf.at[d], par_send.at[d], par_recv.at[d], mate)

    def mix_copy(k):
        return remote(
            dl.at[others[k - 1]], inbox.at[k - 1], mix_send.at[k - 1], mix_recv.at[k - 1],
            {"dp": others[k - 1]},
        )

    def back_copy(d):
        peer = {"ctx": lax.rem(me + n - d, n)}
        return remote(halves.at[d - 1], back.at[d - 1], back_send.at[d - 1], back_recv.at[d - 1], peer)

    def all_copy(k):
        return remote(mine, final.at[k], all_send.at[k - 1], all_recv.at[k - 1], {"dp": others[k - 1]})

    def ring(way, d):
        peer = {"ctx": away(way, d - relay(d))}
        return remote(
            send_buf.at[way, d], recv_buf.at[way, d], ring_send.at[way, d], ring_recv.at[way, d], peer
        )

    def local(d):
        to_mate(d).wait_recv()
        return dw[lax.rem(me + 2 * d, n)].astype(f32) + par_buf[d].astype(f32)

    def arrived(way, first, last):
        total = 0.0
        for d in range(first, min(last, counts[way]) + 1):
            ring(way, d).wait_recv()
            total = total + recv_buf[way, d].astype(f32)
        return total

    def pass_on(way, d):
        total = local(d if way == 0 else 16 - d)
        if d in (3, 6):
            total = total + arrived(way, d + 1, d + 3)
        send_buf[way, d] = total.astype(bf16)
        ring(way, d).start()

    greet(
        [{"ctx": lax.rem(me + d, n)} for d in (1, 2, 4, 6, n - 1, n - 2, n - 4, n - 6)]
        + [{"dp": k} for k in others]
    )
    order = (8, 7, 9, 5, 11, 4, 12, 2, 14, 1, 15, 6, 10, 3, 13, 0)
    for d in order[:3]:
        to_mate(d).start()
    for k in range(1, m):
        mix_copy(k).start()
    for d in order[3:]:
        to_mate(d).start()
    for d in (8, 7, 5, 4):
        for way in range(2):
            if d <= counts[way]:
                pass_on(way, d)
    for way in range(2):
        pass_on(way, 6)
    total = dl[col].astype(f32)
    for k in range(1, m):
        mix_copy(k).wait_recv()
        total = total + inbox[k - 1].astype(f32)
    halves[0] = total[1].astype(bf16)
    halves[1] = total[0].astype(bf16)
    for d in (2, 1):
        back_copy(d).start()
    for d in (2, 1, 3):
        for way in range(2):
            pass_on(way, d)
    total = total[2]
    for d in (2, 1):
        back_copy(d).wait_recv()
        total = total + back[d - 1].astype(f32)
    rope = total[:, 512:]
    rope = rope + pltpu.roll(rope, 64, 1)
    rows = jnp.concatenate([total[:, :512], rope], axis=1).astype(bf16)
    mine[...] = rows
    final[0] = rows
    for k in range(1, m):
        all_copy(k).start()
    total = local(0) + arrived(0, 1, 3) + arrived(1, 1, 3)
    ok[...] = total[:, :width]
    ov[...] = total[:, width:]
    for k in range(1, m):
        all_copy(k).wait_recv()
    for d in range(16):
        to_mate(d).wait_send()
    for way in range(2):
        for d in range(1, counts[way] + 1):
            ring(way, d).wait_send()
    for d in (2, 1):
        back_copy(d).wait_send()
    for k in range(1, m):
        mix_copy(k).wait_send()
        all_copy(k).wait_send()


def reduce(dw, dl):
    sem = pltpu.SemaphoreType.DMA
    width = dw.shape[2] // 2
    return pl.pallas_call(
        reduce_kernel,
        out_shape=(
            jax.ShapeDtypeStruct((16, width), f32),
            jax.ShapeDtypeStruct((16, width), f32),
            jax.ShapeDtypeStruct((16, 8, 640), bf16),
        ),
        in_specs=[VMEM] * 2,
        out_specs=(VMEM,) * 3,
        scratch_shapes=[
            pltpu.VMEM((16, 16, 2 * width), bf16),
            pltpu.VMEM((2, 9, 16, 2 * width), bf16),
            pltpu.VMEM((2, 9, 16, 2 * width), bf16),
            pltpu.VMEM((15, 3, 8, 640), bf16),
            pltpu.VMEM((2, 8, 640), bf16),
            pltpu.VMEM((2, 8, 640), bf16),
            pltpu.VMEM((8, 640), bf16),
            sem((16,)), sem((16,)), sem((2, 9)), sem((2, 9)),
            sem((2,)), sem((2,)), sem((15,)), sem((15,)), sem((15,)), sem((15,)),
        ],
        compiler_params=pltpu.CompilerParams(collective_id=1, has_side_effects=True),
    )(dw, dl)


def place_kernel(wk_ref, wv_ref, rows_ref, ok, ov, olat, orope):
    col = lax.axis_index("dp")
    ok[...] = wk_ref[...]
    ov[...] = wv_ref[...]
    pieces = [rows_ref[lax.rem(col + 16 - j, 16)].astype(f32) for j in range(16)]
    rows = jnp.concatenate(pieces, axis=0)
    olat[...] = rows[:, :512].astype(bf16)
    orope[...] = rows[:, 512:].T[:ROPE].astype(bf16)


def place(wk, wv, rows):
    return pl.pallas_call(
        place_kernel,
        out_shape=(
            jax.ShapeDtypeStruct(wk.shape, f32),
            jax.ShapeDtypeStruct(wv.shape, f32),
            jax.ShapeDtypeStruct((128, 512), bf16),
            jax.ShapeDtypeStruct((ROPE, 128), bf16),
        ),
        in_specs=[VMEM] * 3,
        out_specs=(VMEM,) * 4,
    )(wk, wv, rows)


def on_device(
    q_nope, q_rope, latent, k_rope, w_uk, w_uv, out_grad, log_prob, ref_logp, doc_ids, loss_mask
):
    full, window = gather(
        w_uk, w_uv, latent, k_rope.T, log_prob[None, :], doc_ids[None, :], loss_mask[None, :]
    )
    width = w_uk.shape[1]
    dq_nope, dq_rope, dw, dl = attend(
        window.reshape(384, 640), full.reshape(512, 2 * width + 128), q_nope, q_rope, out_grad,
        ref_logp[None, :],
    )
    dw_uk, dw_uv, d_latent, d_krope = place(*reduce(dw.reshape(32, 16, 2 * width), dl))
    return dq_nope, dq_rope, d_latent, d_krope.T, dw_uk, dw_uv


def solution(mesh):
    both, rows, flat = P("ctx", "dp"), P("ctx", None), P("ctx")
    return jax.shard_map(
        on_device,
        mesh=mesh,
        in_specs=(both, both, rows, rows, both, both, both, flat, P(), flat, flat),
        out_specs=(both, both, rows, rows, both, both),
        check_vma=False,
    )
```

```python
import math

import jax
import jax.numpy as jnp
from jax import lax
from jax.experimental import pallas as pl
from jax.experimental.pallas import tpu as pltpu
from jax.sharding import PartitionSpec as P

NOPE = 128
ROPE = 64
npo_beta = 1.0
MESH = pl.DeviceIdType.MESH
VMEM = pl.BlockSpec(memory_space=pltpu.VMEM)
f32 = jnp.float32
bf16 = jnp.bfloat16


def greet(peers):
    barrier = pltpu.get_barrier_semaphore()
    for peer in peers:
        pl.semaphore_signal(barrier, inc=1, device_id=peer, device_id_type=MESH)
    pl.semaphore_wait(barrier, len(peers))


def remote(src, dst, send, recv, peer):
    return pltpu.make_async_remote_copy(
        src_ref=src, dst_ref=dst, send_sem=send, recv_sem=recv, device_id=peer, device_id_type=MESH
    )


GATHER_SPAN = 2
REDUCE_SPAN = 2


def relay(d, span):
    return span * ((d - 1) // span)


def reach(me, span):
    chips = sorted({1, span} | set(range(1, span + 1)))
    steps = [1] + [2 * c for c in chips]
    return [{"ctx": lax.rem(me + d, 32)} for d in steps + [32 - d for d in steps]]


def gather_kernel(
    uk_ref, uv_ref, lat_ref, rope_ref, logp_ref, doc_ref, mask_ref,
    buf, win, item, near,
    own_sem, ring_send, ring_recv, par_send, par_recv, halo_send, halo_recv,
):
    me = lax.axis_index("ctx")
    n = 32
    core = lax.rem(me, 2)
    partner = me + 1 - 2 * core
    mate = {"ctx": partner}
    counts = (7, 8)
    span = GATHER_SPAN
    width = uk_ref.shape[1]

    item[:, :width] = uk_ref[...]
    item[:, width:2 * width] = uv_ref[...]
    mask = mask_ref[...].astype(f32)
    masked = mask * logp_ref[...]
    high = masked.astype(bf16).astype(f32)
    rest = masked - high
    middle = rest.astype(bf16).astype(f32)
    small = [doc_ref[...].astype(f32), mask, high, middle, rest - middle, jnp.zeros((11, 128), f32)]
    item[:, 2 * width:] = jnp.concatenate(small, axis=0).astype(bf16)
    near[:, :512] = lat_ref[...]
    column = rope_ref[...].astype(f32).T
    near[:, 512:] = jnp.concatenate([column, column], axis=1).astype(bf16)

    def away(way, hops):
        return lax.rem(me + 2 * hops, n) if way == 0 else lax.rem(me + n - 2 * hops, n)

    def origin(base, way, d):
        return lax.rem(base + n - 2 * d, n) if way == 0 else lax.rem(base + 2 * d, n)

    def send(way, d):
        slot = buf.at[origin(me, way, relay(d, span))]
        src = item if relay(d, span) == 0 else slot
        peer = {"ctx": away(way, d - relay(d, span))}
        return remote(src, slot, ring_send.at[way, d], ring_recv.at[way, d], peer)

    def arrival(way, d):
        slot = buf.at[origin(me, way, d)]
        peer = {"ctx": away(1 - way, d - relay(d, span))}
        return remote(slot, slot, ring_send.at[way, d], ring_recv.at[way, d], peer)

    def mate_copy(way, d, base):
        slot = buf.at[origin(base, way, d)]
        src = item if d == 0 else slot
        return remote(src, slot, par_send.at[way, d], par_recv.at[way, d], mate)

    halo = remote(near, win.at[0], halo_send.at[0], halo_recv.at[0], {"ctx": away(0, 1)})
    halo_mate = remote(win.at[2 - 2 * core], win.at[1], halo_send.at[1], halo_recv.at[1], mate)
    ways = (1, 0)

    greet(reach(me, span))
    for d in range(span, 0, -1):
        for way in ways:
            send(way, d).start()
    own = [
        pltpu.make_async_copy(item, buf.at[me], own_sem.at[0]),
        pltpu.make_async_copy(near, win.at[2], own_sem.at[1]),
    ]
    for copy in own:
        copy.start()
    mate_copy(0, 0, me).start()
    halo.start()
    for top in range(span, 8 + span, span):
        if top < 8:
            for way in ways:
                arrival(way, top).wait_recv()
                for d in range(min(top + span, counts[way]), top, -1):
                    send(way, d).start()
        for d in range(top - span + 1, min(top, 8) + 1):
            for way in ways:
                if d <= counts[way]:
                    if d < top or top >= 8:
                        arrival(way, d).wait_recv()
                    mate_copy(way, d, me).start()
    for copy in own:
        copy.wait()
    halo.wait_recv()
    halo_mate.start()
    mate_copy(0, 0, me).wait_send()
    mate_copy(0, 0, partner).wait_recv()
    for d in range(1, 9):
        for way in ways:
            if d <= counts[way]:
                send(way, d).wait_send()
                mate_copy(way, d, me).wait_send()
                mate_copy(way, d, partner).wait_recv()
    halo.wait_send()
    halo_mate.wait_send()
    halo_mate.wait_recv()


def gather(uk, uv, latent, rope, logp, docs, mask):
    sem = pltpu.SemaphoreType.DMA
    total = 2 * uk.shape[1] + 128
    return pl.pallas_call(
        gather_kernel,
        out_shape=(
            jax.ShapeDtypeStruct((32, 16, total), bf16),
            jax.ShapeDtypeStruct((3, 128, 640), bf16),
        ),
        in_specs=[VMEM] * 7,
        out_specs=(VMEM,) * 2,
        scratch_shapes=[
            pltpu.VMEM((16, total), bf16),
            pltpu.VMEM((128, 640), bf16),
            sem((2,)), sem((2, 9)), sem((2, 9)), sem((2, 9)), sem((2, 9)), sem((2,)), sem((2,)),
        ],
        compiler_params=pltpu.CompilerParams(collective_id=0, has_side_effects=True),
    )(uk, uv, latent, rope, logp, docs, mask)


def dot_nt(a, b):
    return lax.dot_general(a, b, (((1,), (1,)), ((), ())), preferred_element_type=f32)


def dot_tn(a, b):
    return lax.dot_general(a, b, (((0,), (0,)), ((), ())), preferred_element_type=f32)


def dot_nn(a, b):
    return jnp.dot(a, b, preferred_element_type=f32)


def small_rows(st_ref, idx):
    return st_ref[pl.ds(pl.multiple_of(idx * 16, 16), 16), :].astype(f32)


def attend_kernel(
    win_ref, uk_ref, uv_ref, q_ref, qr_ref, og_ref, st_ref, base_ref,
    dq_ref, dqr_ref, dw_ref, dl_ref, acc, lat_t, gscale, docs,
):
    step = pl.program_id(0)
    me = lax.axis_index("ctx")
    latent = win_ref[:, :512]

    @pl.when(step == 0)
    def _():
        acc[...] = jnp.zeros_like(acc)
        lat_t[...] = latent.astype(f32).T.astype(bf16)
        every = st_ref[...].astype(f32).reshape(32, 16, 128)
        sums = jnp.sum(jnp.sum(every, axis=0), axis=1, keepdims=True)
        live_count, live_total = sums[1:2], sums[2:3] + sums[3:4] + sums[4:5]
        own = small_rows(st_ref, me)
        gap = npo_beta * (live_total / live_count - base_ref[...])
        weight = 2.0 * (1.0 / (1.0 + jnp.exp(-gap))) * 4096.0 / live_count
        gscale[...] = jnp.broadcast_to(weight * own[1:2], (128, 128)).T
        for t in range(3):
            there = small_rows(st_ref, lax.rem(me + 30 + t, 32))
            docs[t * 128:t * 128 + 128, :] = jnp.broadcast_to(there[0:1], (128, 128)).T

    scale = 1.0 / math.sqrt(NOPE + ROPE)
    key_idx = lax.broadcasted_iota(jnp.int32, (384, 128), 0) - 256
    query_idx = lax.broadcasted_iota(jnp.int32, (384, 128), 1)
    allowed = docs[...] == small_rows(st_ref, me)[0:1]
    allowed = allowed & (key_idx <= query_idx) & (me * 128 + key_idx >= 0)
    low_lane = lax.broadcasted_iota(jnp.int32, (128, 128), 1) < ROPE
    keys = dot_nn(latent, uk_ref[...]).astype(bf16)
    values = dot_nn(latent, uv_ref[...]).astype(bf16)
    key_rope = win_ref[:, 512:]
    query_rope = qr_ref[...].astype(f32)
    scale_col = gscale[...]
    part_k, part_v, rope_q, rope_k = [], [], [], 0.0
    for p in range(2):
        cols = slice(p * 128, p * 128 + 128)
        qn = q_ref[:, cols]
        mine = low_lane if p == 0 else jnp.logical_not(low_lane)
        qr = jnp.where(mine, query_rope, 0.0).astype(bf16)
        kh, vh = keys[:, cols], values[:, cols]
        grad = (scale_col * og_ref[:, cols].astype(f32)).astype(bf16)
        scores = dot_nt(kh, qn) + dot_nt(key_rope, qr)
        scores = jnp.where(allowed, scores * scale, -1e30)
        top = jnp.max(scores, axis=0, keepdims=True)
        expon = jnp.where(allowed, jnp.exp(scores - top), 0.0)
        probs = expon * (1.0 / jnp.sum(expon, axis=0, keepdims=True))
        low = probs.astype(bf16)
        dprob = dot_nt(vh, grad)
        delta = jnp.sum(low.astype(f32) * dprob, axis=0, keepdims=True)
        dscore = (probs * (dprob - delta) * scale).astype(bf16)
        dq_ref[:, cols] = dot_tn(dscore, kh).astype(bf16)
        rope_q.append(dot_tn(dscore, key_rope))
        rope_k = rope_k + dot_nn(dscore, qr)
        part_k.append(dot_nn(dscore, qn).astype(bf16))
        part_v.append(dot_nn(low, grad).astype(bf16))
    dqr_ref[...] = jnp.where(low_lane, rope_q[0], rope_q[1]).astype(bf16)
    part_k = jnp.concatenate(part_k, axis=1)
    part_v = jnp.concatenate(part_v, axis=1)
    acc[:, :512] += dot_nt(part_k, uk_ref[...]) + dot_nt(part_v, uv_ref[...])
    acc[:, 512:] += rope_k
    half = pl.num_programs(0) * 256
    first = pl.multiple_of(step * 256, 256)
    dw_ref[:, pl.ds(first, 256)] = dot_nn(lat_t[...], part_k).astype(bf16)
    dw_ref[:, pl.ds(pl.multiple_of(half + first, 256), 256)] = dot_nn(lat_t[...], part_v).astype(bf16)

    @pl.when(step == pl.num_programs(0) - 1)
    def _():
        for t in range(3):
            dl_ref[:, t] = acc[t * 128:t * 128 + 128, :].reshape(16, 8, 640).astype(bf16)


def attend(window, full, q_nope, q_rope, out_grad, base):
    width = q_nope.shape[1]

    def cols(rows, block):
        return pl.BlockSpec((rows, block), lambda i: (0, i))

    def whole(shape):
        return pl.BlockSpec(shape, lambda i: (0,) * len(shape))

    return pl.pallas_call(
        attend_kernel,
        grid=(width // 256,),
        out_shape=(
            jax.ShapeDtypeStruct(q_nope.shape, bf16),
            jax.ShapeDtypeStruct(q_rope.shape, bf16),
            jax.ShapeDtypeStruct((512, 2 * width), bf16),
            jax.ShapeDtypeStruct((16, 3, 8, 640), bf16),
        ),
        in_specs=[
            whole((384, 640)), cols(512, 256), pl.BlockSpec((512, 256), lambda i: (0, i + width // 256)),
            cols(128, 256), cols(128, 128), cols(128, 256),
            pl.BlockSpec((512, 128), lambda i: (0, width // 64)), whole((1, 1)),
        ],
        out_specs=(cols(128, 256), cols(128, 128), whole((512, 2 * width)), whole((16, 3, 8, 640))),
        scratch_shapes=[
            pltpu.VMEM((384, 640), f32), pltpu.VMEM((512, 384), bf16), pltpu.VMEM((128, 128), f32),
            pltpu.VMEM((384, 128), f32),
        ],
        compiler_params=pltpu.CompilerParams(dimension_semantics=("arbitrary",)),
    )(window, full, full, q_nope, q_rope, out_grad, full, base)


def reduce_kernel(
    dw, dl, ok, ov, final, par_buf, recv_buf, send_buf, inbox, halves, back, mine,
    par_send, par_recv, ring_send, ring_recv, back_send, back_recv, mix_send, mix_recv, all_send, all_recv,
):
    me, col = lax.axis_index("ctx"), lax.axis_index("dp")
    n, m = 32, 16
    core = lax.rem(me, 2)
    partner = me + 1 - 2 * core
    mate = {"ctx": partner}
    counts = (8, 7)
    span = REDUCE_SPAN
    others = [lax.rem(col + k, m) for k in range(1, m)]
    width = ok.shape[1]

    def away(way, hops):
        return lax.rem(me + 2 * hops, n) if way == 0 else lax.rem(me + n - 2 * hops, n)

    def to_mate(d):
        src = dw.at[lax.rem(partner + 2 * d, n)]
        return remote(src, par_buf.at[d], par_send.at[d], par_recv.at[d], mate)

    def mix_copy(k):
        return remote(
            dl.at[others[k - 1]], inbox.at[k - 1], mix_send.at[k - 1], mix_recv.at[k - 1],
            {"dp": others[k - 1]},
        )

    def back_copy(d):
        peer = {"ctx": lax.rem(me + n - d, n)}
        return remote(halves.at[d - 1], back.at[d - 1], back_send.at[d - 1], back_recv.at[d - 1], peer)

    def all_copy(k):
        return remote(mine, final.at[k], all_send.at[k - 1], all_recv.at[k - 1], {"dp": others[k - 1]})

    def ring(way, d):
        peer = {"ctx": away(way, d - relay(d, span))}
        return remote(
            send_buf.at[way, d], recv_buf.at[way, d], ring_send.at[way, d], ring_recv.at[way, d], peer
        )

    def local(d):
        to_mate(d).wait_recv()
        return dw[lax.rem(me + 2 * d, n)].astype(f32) + par_buf[d].astype(f32)

    def arrived(way, first, last):
        total = 0.0
        for d in range(first, min(last, counts[way]) + 1):
            ring(way, d).wait_recv()
            total = total + recv_buf[way, d].astype(f32)
        return total

    def pass_on(way, d):
        total = local(d if way == 0 else 16 - d)
        if d % span == 0 and d < 8:
            total = total + arrived(way, d + 1, d + span)
        send_buf[way, d] = total.astype(bf16)
        ring(way, d).start()

    greet(
        reach(me, span) + [{"dp": k} for k in others]
    )
    order = (8, 7, 9, 5, 11, 4, 12, 2, 14, 1, 15, 6, 10, 3, 13, 0)
    for d in order[:3]:
        to_mate(d).start()
    for k in range(1, m):
        mix_copy(k).start()
    for d in order[3:]:
        to_mate(d).start()
    plan = {1: (8, 7, 6, 5, 4, 3, 2, 1), 2: (8, 7, 5, 6, 3, 4, 1, 2), 3: (8, 7, 5, 4, 6, 2, 1, 3)}[span]
    for d in plan[:4]:
        for way in range(2):
            if d <= counts[way]:
                pass_on(way, d)
    total = dl[col].astype(f32)
    for k in range(1, m):
        mix_copy(k).wait_recv()
        total = total + inbox[k - 1].astype(f32)
    halves[0] = total[1].astype(bf16)
    halves[1] = total[0].astype(bf16)
    for d in (2, 1):
        back_copy(d).start()
    for d in plan[4:]:
        for way in range(2):
            pass_on(way, d)
    total = total[2]
    for d in (2, 1):
        back_copy(d).wait_recv()
        total = total + back[d - 1].astype(f32)
    rope = total[:, 512:]
    rope = rope + pltpu.roll(rope, 64, 1)
    rows = jnp.concatenate([total[:, :512], rope], axis=1).astype(bf16)
    mine[...] = rows
    final[0] = rows
    for k in range(1, m):
        all_copy(k).start()
    total = local(0) + arrived(0, 1, span) + arrived(1, 1, span)
    ok[...] = total[:, :width]
    ov[...] = total[:, width:]
    for k in range(1, m):
        all_copy(k).wait_recv()
    for d in range(16):
        to_mate(d).wait_send()
    for way in range(2):
        for d in range(1, counts[way] + 1):
            ring(way, d).wait_send()
    for d in (2, 1):
        back_copy(d).wait_send()
    for k in range(1, m):
        mix_copy(k).wait_send()
        all_copy(k).wait_send()


def reduce(dw, dl):
    sem = pltpu.SemaphoreType.DMA
    width = dw.shape[2] // 2
    return pl.pallas_call(
        reduce_kernel,
        out_shape=(
            jax.ShapeDtypeStruct((16, width), f32),
            jax.ShapeDtypeStruct((16, width), f32),
            jax.ShapeDtypeStruct((16, 8, 640), bf16),
        ),
        in_specs=[VMEM] * 2,
        out_specs=(VMEM,) * 3,
        scratch_shapes=[
            pltpu.VMEM((16, 16, 2 * width), bf16),
            pltpu.VMEM((2, 9, 16, 2 * width), bf16),
            pltpu.VMEM((2, 9, 16, 2 * width), bf16),
            pltpu.VMEM((15, 3, 8, 640), bf16),
            pltpu.VMEM((2, 8, 640), bf16),
            pltpu.VMEM((2, 8, 640), bf16),
            pltpu.VMEM((8, 640), bf16),
            sem((16,)), sem((16,)), sem((2, 9)), sem((2, 9)),
            sem((2,)), sem((2,)), sem((15,)), sem((15,)), sem((15,)), sem((15,)),
        ],
        compiler_params=pltpu.CompilerParams(collective_id=1, has_side_effects=True),
    )(dw, dl)


def place_kernel(wk_ref, wv_ref, rows_ref, ok, ov, olat, orope):
    col = lax.axis_index("dp")
    ok[...] = wk_ref[...]
    ov[...] = wv_ref[...]
    pieces = [rows_ref[lax.rem(col + 16 - j, 16)].astype(f32) for j in range(16)]
    rows = jnp.concatenate(pieces, axis=0)
    olat[...] = rows[:, :512].astype(bf16)
    orope[...] = rows[:, 512:].T[:ROPE].astype(bf16)


def place(wk, wv, rows):
    return pl.pallas_call(
        place_kernel,
        out_shape=(
            jax.ShapeDtypeStruct(wk.shape, f32),
            jax.ShapeDtypeStruct(wv.shape, f32),
            jax.ShapeDtypeStruct((128, 512), bf16),
            jax.ShapeDtypeStruct((ROPE, 128), bf16),
        ),
        in_specs=[VMEM] * 3,
        out_specs=(VMEM,) * 4,
    )(wk, wv, rows)


def on_device(
    q_nope, q_rope, latent, k_rope, w_uk, w_uv, out_grad, log_prob, ref_logp, doc_ids, loss_mask
):
    full, window = gather(
        w_uk, w_uv, latent, k_rope.T, log_prob[None, :], doc_ids[None, :], loss_mask[None, :]
    )
    width = w_uk.shape[1]
    dq_nope, dq_rope, dw, dl = attend(
        window.reshape(384, 640), full.reshape(512, 2 * width + 128), q_nope, q_rope, out_grad,
        ref_logp[None, :],
    )
    dw_uk, dw_uv, d_latent, d_krope = place(*reduce(dw.reshape(32, 16, 2 * width), dl))
    return dq_nope, dq_rope, d_latent, d_krope.T, dw_uk, dw_uv


def solution(mesh):
    both, rows, flat = P("ctx", "dp"), P("ctx", None), P("ctx")
    return jax.shard_map(
        on_device,
        mesh=mesh,
        in_specs=(both, both, rows, rows, both, both, both, flat, P(), flat, flat),
        out_specs=(both, both, rows, rows, both, both),
        check_vma=False,
    )
```

```python
import math

import jax
import jax.numpy as jnp
from jax import lax
from jax.experimental import pallas as pl
from jax.experimental.pallas import tpu as pltpu
from jax.sharding import PartitionSpec as P

NOPE = 128
ROPE = 64
npo_beta = 1.0
MESH = pl.DeviceIdType.MESH
VMEM = pl.BlockSpec(memory_space=pltpu.VMEM)
f32 = jnp.float32
bf16 = jnp.bfloat16


def announce(peers):
    barrier = pltpu.get_barrier_semaphore()
    for peer in peers:
        pl.semaphore_signal(barrier, inc=1, device_id=peer, device_id_type=MESH)


def await_peers(peers):
    pl.semaphore_wait(pltpu.get_barrier_semaphore(), len(peers))


def greet(peers):
    announce(peers)
    await_peers(peers)


def remote(src, dst, send, recv, peer):
    return pltpu.make_async_remote_copy(
        src_ref=src, dst_ref=dst, send_sem=send, recv_sem=recv, device_id=peer, device_id_type=MESH
    )


GATHER_SPAN = 2
REDUCE_SPAN = 2


def relay(d, span):
    return span * ((d - 1) // span)


def reach(me, span):
    chips = sorted({1, span} | set(range(1, span + 1)))
    steps = [1] + [2 * c for c in chips]
    return [{"ctx": lax.rem(me + d, 32)} for d in steps + [32 - d for d in steps]]


def gather_kernel(
    uk_ref, uv_ref, lat_ref, rope_ref, logp_ref, doc_ref, mask_ref,
    buf, win, item, near,
    own_sem, ring_send, ring_recv, par_send, par_recv, halo_send, halo_recv,
):
    me = lax.axis_index("ctx")
    n = 32
    core = lax.rem(me, 2)
    partner = me + 1 - 2 * core
    mate = {"ctx": partner}
    counts = (7, 8)
    span = GATHER_SPAN
    width = uk_ref.shape[1]

    peers = reach(me, span)
    announce(peers)
    item[:, :width] = uk_ref[...]
    item[:, width:2 * width] = uv_ref[...]
    mask = mask_ref[...].astype(f32)
    masked = mask * logp_ref[...]
    high = masked.astype(bf16).astype(f32)
    rest = masked - high
    middle = rest.astype(bf16).astype(f32)
    small = [doc_ref[...].astype(f32), mask, high, middle, rest - middle, jnp.zeros((11, 128), f32)]
    item[:, 2 * width:] = jnp.concatenate(small, axis=0).astype(bf16)
    near[:, :512] = lat_ref[...]
    column = rope_ref[...].astype(f32).T
    near[:, 512:] = jnp.concatenate([column, column], axis=1).astype(bf16)

    def away(way, hops):
        return lax.rem(me + 2 * hops, n) if way == 0 else lax.rem(me + n - 2 * hops, n)

    def origin(base, way, d):
        return lax.rem(base + n - 2 * d, n) if way == 0 else lax.rem(base + 2 * d, n)

    def send(way, d):
        slot = buf.at[origin(me, way, relay(d, span))]
        src = item if relay(d, span) == 0 else slot
        peer = {"ctx": away(way, d - relay(d, span))}
        return remote(src, slot, ring_send.at[way, d], ring_recv.at[way, d], peer)

    def arrival(way, d):
        slot = buf.at[origin(me, way, d)]
        peer = {"ctx": away(1 - way, d - relay(d, span))}
        return remote(slot, slot, ring_send.at[way, d], ring_recv.at[way, d], peer)

    def mate_copy(way, d, base):
        slot = buf.at[origin(base, way, d)]
        src = item if d == 0 else slot
        return remote(src, slot, par_send.at[way, d], par_recv.at[way, d], mate)

    halo = remote(near, win.at[0], halo_send.at[0], halo_recv.at[0], {"ctx": away(0, 1)})
    halo_mate = remote(win.at[2 - 2 * core], win.at[1], halo_send.at[1], halo_recv.at[1], mate)
    ways = (1, 0)

    await_peers(peers)
    for d in range(span, 0, -1):
        for way in ways:
            send(way, d).start()
    own = [
        pltpu.make_async_copy(item, buf.at[me], own_sem.at[0]),
        pltpu.make_async_copy(near, win.at[2], own_sem.at[1]),
    ]
    for copy in own:
        copy.start()
    mate_copy(0, 0, me).start()
    halo.start()
    for top in range(span, 8 + span, span):
        if top < 8:
            for way in ways:
                arrival(way, top).wait_recv()
                for d in range(min(top + span, counts[way]), top, -1):
                    send(way, d).start()
        for d in range(top - span + 1, min(top, 8) + 1):
            for way in ways:
                if d <= counts[way]:
                    if d < top or top >= 8:
                        arrival(way, d).wait_recv()
                    mate_copy(way, d, me).start()
    for copy in own:
        copy.wait()
    halo.wait_recv()
    halo_mate.start()
    mate_copy(0, 0, me).wait_send()
    mate_copy(0, 0, partner).wait_recv()
    for d in range(1, 9):
        for way in ways:
            if d <= counts[way]:
                send(way, d).wait_send()
                mate_copy(way, d, me).wait_send()
                mate_copy(way, d, partner).wait_recv()
    halo.wait_send()
    halo_mate.wait_send()
    halo_mate.wait_recv()


def gather(uk, uv, latent, rope, logp, docs, mask):
    sem = pltpu.SemaphoreType.DMA
    total = 2 * uk.shape[1] + 128
    return pl.pallas_call(
        gather_kernel,
        out_shape=(
            jax.ShapeDtypeStruct((32, 16, total), bf16),
            jax.ShapeDtypeStruct((3, 128, 640), bf16),
        ),
        in_specs=[VMEM] * 7,
        out_specs=(VMEM,) * 2,
        scratch_shapes=[
            pltpu.VMEM((16, total), bf16),
            pltpu.VMEM((128, 640), bf16),
            sem((2,)), sem((2, 9)), sem((2, 9)), sem((2, 9)), sem((2, 9)), sem((2,)), sem((2,)),
        ],
        compiler_params=pltpu.CompilerParams(collective_id=0, has_side_effects=True),
    )(uk, uv, latent, rope, logp, docs, mask)


def dot_nt(a, b):
    return lax.dot_general(a, b, (((1,), (1,)), ((), ())), preferred_element_type=f32)


def dot_tn(a, b):
    return lax.dot_general(a, b, (((0,), (0,)), ((), ())), preferred_element_type=f32)


def dot_nn(a, b):
    return jnp.dot(a, b, preferred_element_type=f32)


def small_rows(st_ref, idx):
    return st_ref[pl.ds(pl.multiple_of(idx * 16, 16), 16), :].astype(f32)


def attend_kernel(
    win_ref, uk_ref, uv_ref, q_ref, qr_ref, og_ref, st_ref, base_ref,
    dq_ref, dqr_ref, dw_ref, dl_ref, acc, lat_t, gscale, docs,
):
    step = pl.program_id(0)
    me = lax.axis_index("ctx")
    latent = win_ref[:, :512]

    @pl.when(step == 0)
    def _():
        acc[...] = jnp.zeros_like(acc)
        lat_t[...] = latent.astype(f32).T.astype(bf16)
        every = st_ref[...].astype(f32).reshape(32, 16, 128)
        sums = jnp.sum(jnp.sum(every, axis=0), axis=1, keepdims=True)
        live_count, live_total = sums[1:2], sums[2:3] + sums[3:4] + sums[4:5]
        own = small_rows(st_ref, me)
        gap = npo_beta * (live_total / live_count - base_ref[...])
        weight = 2.0 * (1.0 / (1.0 + jnp.exp(-gap))) * 4096.0 / live_count
        gscale[...] = jnp.broadcast_to(weight * own[1:2], (128, 128)).T
        for t in range(3):
            there = small_rows(st_ref, lax.rem(me + 30 + t, 32))
            docs[t * 128:t * 128 + 128, :] = jnp.broadcast_to(there[0:1], (128, 128)).T

    scale = 1.0 / math.sqrt(NOPE + ROPE)
    key_idx = lax.broadcasted_iota(jnp.int32, (384, 128), 0) - 256
    query_idx = lax.broadcasted_iota(jnp.int32, (384, 128), 1)
    allowed = docs[...] == small_rows(st_ref, me)[0:1]
    allowed = allowed & (key_idx <= query_idx) & (me * 128 + key_idx >= 0)
    low_lane = lax.broadcasted_iota(jnp.int32, (128, 128), 1) < ROPE
    keys = dot_nn(latent, uk_ref[...]).astype(bf16)
    values = dot_nn(latent, uv_ref[...]).astype(bf16)
    key_rope = win_ref[:, 512:]
    query_rope = qr_ref[...].astype(f32)
    scale_col = gscale[...]
    part_k, part_v, rope_q, rope_k = [], [], [], 0.0
    for p in range(2):
        cols = slice(p * 128, p * 128 + 128)
        qn = q_ref[:, cols]
        mine = low_lane if p == 0 else jnp.logical_not(low_lane)
        qr = jnp.where(mine, query_rope, 0.0).astype(bf16)
        kh, vh = keys[:, cols], values[:, cols]
        grad = (scale_col * og_ref[:, cols].astype(f32)).astype(bf16)
        scores = dot_nt(kh, qn) + dot_nt(key_rope, qr)
        scores = jnp.where(allowed, scores * scale, -1e30)
        top = jnp.max(scores, axis=0, keepdims=True)
        expon = jnp.where(allowed, jnp.exp(scores - top), 0.0)
        probs = expon * (1.0 / jnp.sum(expon, axis=0, keepdims=True))
        low = probs.astype(bf16)
        dprob = dot_nt(vh, grad)
        delta = jnp.sum(low.astype(f32) * dprob, axis=0, keepdims=True)
        dscore = (probs * (dprob - delta) * scale).astype(bf16)
        dq_ref[:, cols] = dot_tn(dscore, kh).astype(bf16)
        rope_q.append(dot_tn(dscore, key_rope))
        rope_k = rope_k + dot_nn(dscore, qr)
        part_k.append(dot_nn(dscore, qn).astype(bf16))
        part_v.append(dot_nn(low, grad).astype(bf16))
    dqr_ref[...] = jnp.where(low_lane, rope_q[0], rope_q[1]).astype(bf16)
    part_k = jnp.concatenate(part_k, axis=1)
    part_v = jnp.concatenate(part_v, axis=1)
    acc[:, :512] += dot_nt(part_k, uk_ref[...]) + dot_nt(part_v, uv_ref[...])
    acc[:, 512:] += rope_k
    half = pl.num_programs(0) * 256
    first = pl.multiple_of(step * 256, 256)
    dw_ref[:, pl.ds(first, 256)] = dot_nn(lat_t[...], part_k).astype(bf16)
    dw_ref[:, pl.ds(pl.multiple_of(half + first, 256), 256)] = dot_nn(lat_t[...], part_v).astype(bf16)

    @pl.when(step == pl.num_programs(0) - 1)
    def _():
        for t in range(3):
            dl_ref[:, t] = acc[t * 128:t * 128 + 128, :].reshape(16, 8, 640).astype(bf16)


def attend(window, full, q_nope, q_rope, out_grad, base):
    width = q_nope.shape[1]

    def cols(rows, block):
        return pl.BlockSpec((rows, block), lambda i: (0, i))

    def whole(shape):
        return pl.BlockSpec(shape, lambda i: (0,) * len(shape))

    return pl.pallas_call(
        attend_kernel,
        grid=(width // 256,),
        out_shape=(
            jax.ShapeDtypeStruct(q_nope.shape, bf16),
            jax.ShapeDtypeStruct(q_rope.shape, bf16),
            jax.ShapeDtypeStruct((512, 2 * width), bf16),
            jax.ShapeDtypeStruct((16, 3, 8, 640), bf16),
        ),
        in_specs=[
            whole((384, 640)), cols(512, 256), pl.BlockSpec((512, 256), lambda i: (0, i + width // 256)),
            cols(128, 256), cols(128, 128), cols(128, 256),
            pl.BlockSpec((512, 128), lambda i: (0, width // 64)), whole((1, 1)),
        ],
        out_specs=(cols(128, 256), cols(128, 128), whole((512, 2 * width)), whole((16, 3, 8, 640))),
        scratch_shapes=[
            pltpu.VMEM((384, 640), f32), pltpu.VMEM((512, 384), bf16), pltpu.VMEM((128, 128), f32),
            pltpu.VMEM((384, 128), f32),
        ],
        compiler_params=pltpu.CompilerParams(dimension_semantics=("arbitrary",)),
    )(window, full, full, q_nope, q_rope, out_grad, full, base)


def reduce_kernel(
    dw, dl, ok, ov, final, par_buf, recv_buf, send_buf, inbox, halves, back, mine,
    par_send, par_recv, ring_send, ring_recv, back_send, back_recv, mix_send, mix_recv, all_send, all_recv,
):
    me, col = lax.axis_index("ctx"), lax.axis_index("dp")
    n, m = 32, 16
    core = lax.rem(me, 2)
    partner = me + 1 - 2 * core
    mate = {"ctx": partner}
    counts = (8, 7)
    span = REDUCE_SPAN
    others = [lax.rem(col + k, m) for k in range(1, m)]
    width = ok.shape[1]

    def away(way, hops):
        return lax.rem(me + 2 * hops, n) if way == 0 else lax.rem(me + n - 2 * hops, n)

    def to_mate(d):
        src = dw.at[lax.rem(partner + 2 * d, n)]
        return remote(src, par_buf.at[d], par_send.at[d], par_recv.at[d], mate)

    def mix_copy(k):
        return remote(
            dl.at[others[k - 1]], inbox.at[k - 1], mix_send.at[k - 1], mix_recv.at[k - 1],
            {"dp": others[k - 1]},
        )

    def back_copy(d):
        peer = {"ctx": lax.rem(me + n - d, n)}
        return remote(halves.at[d - 1], back.at[d - 1], back_send.at[d - 1], back_recv.at[d - 1], peer)

    def all_copy(k):
        return remote(mine, final.at[k], all_send.at[k - 1], all_recv.at[k - 1], {"dp": others[k - 1]})

    def ring(way, d):
        peer = {"ctx": away(way, d - relay(d, span))}
        return remote(
            send_buf.at[way, d], recv_buf.at[way, d], ring_send.at[way, d], ring_recv.at[way, d], peer
        )

    def local(d):
        to_mate(d).wait_recv()
        return dw[lax.rem(me + 2 * d, n)].astype(f32) + par_buf[d].astype(f32)

    def arrived(way, first, last):
        total = 0.0
        for d in range(first, min(last, counts[way]) + 1):
            ring(way, d).wait_recv()
            total = total + recv_buf[way, d].astype(f32)
        return total

    def pass_on(way, d):
        total = local(d if way == 0 else 16 - d)
        if d % span == 0 and d < 8:
            total = total + arrived(way, d + 1, d + span)
        send_buf[way, d] = total.astype(bf16)
        ring(way, d).start()

    greet(
        reach(me, span) + [{"dp": k} for k in others]
    )
    order = (8, 7, 9, 5, 11, 6, 10, 3, 13, 4, 12, 1, 15, 2, 14, 0)
    for d in order[:3]:
        to_mate(d).start()
    for k in range(1, m):
        mix_copy(k).start()
    for d in order[3:]:
        to_mate(d).start()
    plan = {1: (8, 7, 6, 5, 4, 3, 2, 1), 2: (8, 7, 5, 6, 3, 4, 1, 2), 3: (8, 7, 5, 4, 6, 2, 1, 3)}[span]
    for d in plan[:4]:
        for way in range(2):
            if d <= counts[way]:
                pass_on(way, d)
    total = dl[col].astype(f32)
    for k in range(1, m):
        mix_copy(k).wait_recv()
        total = total + inbox[k - 1].astype(f32)
    halves[0] = total[1].astype(bf16)
    halves[1] = total[0].astype(bf16)
    for d in (2, 1):
        back_copy(d).start()
    for d in plan[4:6]:
        for way in range(2):
            pass_on(way, d)
    total = total[2]
    for d in (2, 1):
        back_copy(d).wait_recv()
        total = total + back[d - 1].astype(f32)
    rope = total[:, 512:]
    rope = rope + pltpu.roll(rope, 64, 1)
    rows = jnp.concatenate([total[:, :512], rope], axis=1).astype(bf16)
    mine[...] = rows
    final[0] = rows
    for k in range(1, m):
        all_copy(k).start()
    for d in plan[6:]:
        for way in range(2):
            pass_on(way, d)
    total = local(0) + arrived(0, 1, span) + arrived(1, 1, span)
    ok[...] = total[:, :width]
    ov[...] = total[:, width:]
    for k in range(1, m):
        all_copy(k).wait_recv()
    for d in range(16):
        to_mate(d).wait_send()
    for way in range(2):
        for d in range(1, counts[way] + 1):
            ring(way, d).wait_send()
    for d in (2, 1):
        back_copy(d).wait_send()
    for k in range(1, m):
        mix_copy(k).wait_send()
        all_copy(k).wait_send()


def reduce(dw, dl):
    sem = pltpu.SemaphoreType.DMA
    width = dw.shape[2] // 2
    return pl.pallas_call(
        reduce_kernel,
        out_shape=(
            jax.ShapeDtypeStruct((16, width), f32),
            jax.ShapeDtypeStruct((16, width), f32),
            jax.ShapeDtypeStruct((16, 8, 640), bf16),
        ),
        in_specs=[VMEM] * 2,
        out_specs=(VMEM,) * 3,
        scratch_shapes=[
            pltpu.VMEM((16, 16, 2 * width), bf16),
            pltpu.VMEM((2, 9, 16, 2 * width), bf16),
            pltpu.VMEM((2, 9, 16, 2 * width), bf16),
            pltpu.VMEM((15, 3, 8, 640), bf16),
            pltpu.VMEM((2, 8, 640), bf16),
            pltpu.VMEM((2, 8, 640), bf16),
            pltpu.VMEM((8, 640), bf16),
            sem((16,)), sem((16,)), sem((2, 9)), sem((2, 9)),
            sem((2,)), sem((2,)), sem((15,)), sem((15,)), sem((15,)), sem((15,)),
        ],
        compiler_params=pltpu.CompilerParams(collective_id=1, has_side_effects=True),
    )(dw, dl)


def place_kernel(wk_ref, wv_ref, rows_ref, ok, ov, olat, orope):
    col = lax.axis_index("dp")
    ok[...] = wk_ref[...]
    ov[...] = wv_ref[...]
    pieces = [rows_ref[lax.rem(col + 16 - j, 16)].astype(f32) for j in range(16)]
    rows = jnp.concatenate(pieces, axis=0)
    olat[...] = rows[:, :512].astype(bf16)
    orope[...] = rows[:, 512:].T[:ROPE].astype(bf16)


def place(wk, wv, rows):
    return pl.pallas_call(
        place_kernel,
        out_shape=(
            jax.ShapeDtypeStruct(wk.shape, f32),
            jax.ShapeDtypeStruct(wv.shape, f32),
            jax.ShapeDtypeStruct((128, 512), bf16),
            jax.ShapeDtypeStruct((ROPE, 128), bf16),
        ),
        in_specs=[VMEM] * 3,
        out_specs=(VMEM,) * 4,
    )(wk, wv, rows)


def on_device(
    q_nope, q_rope, latent, k_rope, w_uk, w_uv, out_grad, log_prob, ref_logp, doc_ids, loss_mask
):
    full, window = gather(
        w_uk, w_uv, latent, k_rope.T, log_prob[None, :], doc_ids[None, :], loss_mask[None, :]
    )
    width = w_uk.shape[1]
    dq_nope, dq_rope, dw, dl = attend(
        window.reshape(384, 640), full.reshape(512, 2 * width + 128), q_nope, q_rope, out_grad,
        ref_logp[None, :],
    )
    dw_uk, dw_uv, d_latent, d_krope = place(*reduce(dw.reshape(32, 16, 2 * width), dl))
    return dq_nope, dq_rope, d_latent, d_krope.T, dw_uk, dw_uv


def solution(mesh):
    both, rows, flat = P("ctx", "dp"), P("ctx", None), P("ctx")
    return jax.shard_map(
        on_device,
        mesh=mesh,
        in_specs=(both, both, rows, rows, both, both, both, flat, P(), flat, flat),
        out_specs=(both, both, rows, rows, both, both),
        check_vma=False,
    )
```
